32 devices in a mesh: runs: 2 (over y), lon: 4 (over x, core), lat: 4 (over z).
Axes of the slice: x: 2, y: 2, z: 4, core: 2. Of those that a mesh axis runs over, the one named last changes fastest.
Arguments:
- latent: bfloat16 [8, 24, 48, 512], P('runs', 'lat', 'lon'), parts along dimension 0, may hold values from -16 to 16
- cotangent: bfloat16 [8, 24, 48, 512], P('runs', 'lat', 'lon'), parts along dimension 0, may hold values from -6 to 6
- mask_ids: int32 [8, 24, 48], P('runs', 'lat', 'lon'), parts along dimension 0, may hold values from 0 to 1
- position_bias: float32 [8, 37], replicated, may hold values from -2 to 302
- norm_gain: float32 [512], replicated, may hold values from 0.1 to 1.9
- w_qkv: bfloat16 [512, 1536], replicated, may hold values from -0.25 to 0.25
- qkv_down: bfloat16 [16, 512], replicated, may hold values from -0.25 to 0.25
- qkv_up: bfloat16 [16, 1536], replicated, may hold values from -0.75 to 0.75
- w_proj: bfloat16 [512, 512], replicated, may hold values from -0.25 to 0.25
- proj_down: bfloat16 [16, 512], replicated, may hold values from -0.25 to 0.25
- proj_up: bfloat16 [16, 512], replicated, may hold values from -0.75 to 0.75
Outputs:
- output: bfloat16 [8, 24, 48, 512], P('runs', 'lat', 'lon'), parts along dimension 0
- latent_grad: bfloat16 [8, 24, 48, 512], P('runs', 'lat', 'lon'), parts along dimension 0
- qkv_down_grad: float32 [32, 512], P('runs'), parts along dimension 0
- qkv_up_grad: float32 [32, 1536], P('runs'), parts along dimension 0
- proj_down_grad: float32 [32, 512], P('runs'), parts along dimension 0
- proj_up_grad: float32 [32, 512], P('runs'), parts along dimension 0
The draws below stay inside these ranges and needn't reach their ends.
There are 2 independent parts, one for each index of `runs`. The reference program is written for one: setup_inputs(seed, part) draws one part's arguments, and reference() takes and returns one part's arrays. A program takes and returns all parts, laid end to end along the dimension named above; an argument that names none is the same for every part. Nothing has to cross between parts.
All inputs are finite; a program needn't handle non-finite values.
Results may differ from the reference program's by a relative error of at most 0.011.
Values may be sent and summed in bfloat16 or wider, within the bound.
A program may use at most 64 MiB of HBM per device.

```python
import math
import jax
import jax.numpy as jnp
from jax import lax

D = 512
HEADS = 8
LEVELS = 4
RANK = 16
WIN_LEV = 2
WIN_LAT = 6
WIN_LON = 12
LAT = 24
LON = 48
TOKENS = 4608
BIAS_COLS = 37


def draw_latent(key, part):
    key_base = jax.random.fold_in(key, 0)
    shape = (LEVELS, LAT, LON, D)
    values = jax.random.normal(key_base, shape, jnp.float32)
    return jnp.clip(values, -16.0, 16.0).astype(jnp.bfloat16)


def draw_position_bias(key, part):
    key_base = jax.random.fold_in(jax.random.fold_in(key, 17), 0)
    base = jax.random.uniform(key_base, (HEADS, BIAS_COLS), jnp.float32, -2.0, 2.0)
    values = base
    return values


def plant(result, key, least, largest):
    index_at = [jax.random.randint(jax.random.fold_in(key, axis), (), 0, length) for axis, length in enumerate(result.shape)]
    widest = result.shape.index(max(result.shape))
    neighbour = index_at[:widest] + [(index_at[widest] + 1) % result.shape[widest]] + index_at[widest + 1:]
    return result.at[tuple(index_at)].set(least).at[tuple(neighbour)].set(largest)


def level_of(rng, dims, cuts, smallest, top_value):
    def one(axis_at, shards_of):
        heights = jax.random.uniform(jax.random.fold_in(jax.random.fold_in(rng, 6), axis_at), (shards_of,), jnp.float32, smallest / len(cuts), top_value / len(cuts))
        return jnp.repeat(jnp.exp(heights), dims[axis_at] // shards_of).reshape((-1,) + (1,) * (len(dims) - axis_at - 1))

    gain = one(*cuts[0])
    for cut in cuts[1:]:
        gain = gain * one(*cut)
    return gain


def noise(stream_key, extent, deviation, most, shards=(), kind=jnp.bfloat16):
    values = deviation * jax.random.normal(stream_key, extent, jnp.float32)
    if shards:
        values = values * level_of(stream_key, extent, shards, -0.22, 0.18)
    return jnp.clip(values, -most, most).astype(kind)


def setup_inputs(seed: int = 0, part: int = 0) -> dict:
    splits = jax.random.split(jax.random.key(seed), 12)
    own_keys = jax.random.split(jax.random.fold_in(splits[11], part), 12)
    return {
        "latent": draw_latent(jax.random.fold_in(jax.random.fold_in(splits[11], part), 71), part),
        "cotangent": noise(own_keys[1], (LEVELS, LAT, LON, D), 1.0, 6.0, ((1, 4), (2, 4))),
        "mask_ids": plant(jax.random.randint(own_keys[2], (LEVELS, LAT, LON), 0, 2), jax.random.fold_in(own_keys[2], 1), 0, 1).astype(jnp.int32),
        "position_bias": draw_position_bias(jax.random.fold_in(splits[11], 71), part),
        "norm_gain": jnp.clip(1.0 + 0.18 * jax.random.normal(splits[4], (D,), jnp.float32), 0.1, 1.9),
        "w_qkv": noise(splits[5], (D, 3 * D), D ** -0.5, 0.25),
        "qkv_down": noise(splits[6], (RANK, D), D ** -0.5, 0.25),
        "qkv_up": noise(splits[7], (RANK, 3 * D), (4 * RANK) ** -0.5, 0.75),
        "w_proj": noise(splits[8], (D, D), D ** -0.5, 0.25),
        "proj_down": noise(splits[9], (RANK, D), D ** -0.5, 0.25),
        "proj_up": noise(splits[10], (RANK, D), (4 * RANK) ** -0.5, 0.75),
    }


epsilon = 1e-05
masked_value = -1e+30

def widen(array_in):
    return array_in.astype(jnp.float32)

def dot_rows(left_side, right_side):
    return lax.dot_general(widen(left_side), widen(right_side), (((1,), (1,)), ((), ())))

def dot_cols(left_side, right_side):
    return lax.dot_general(widen(left_side), widen(right_side), (((0,), (0,)), ((), ())))

def window_bias(position_bias):
    window_size = WIN_LEV * WIN_LAT * WIN_LON
    places = jnp.arange(window_size, dtype=jnp.int32)
    level_pos = places // (WIN_LAT * WIN_LON)
    lat_pos = places // WIN_LON % WIN_LAT
    lon_pos = places % WIN_LON
    level_col = level_pos[:, None] - level_pos[None, :] + WIN_LEV - 1
    lat_col = lat_pos[:, None] - lat_pos[None, :] + 2 * WIN_LEV - 1 + WIN_LAT - 1
    lon_col = lon_pos[:, None] - lon_pos[None, :] + 2 * WIN_LEV + 2 * WIN_LAT - 2 + WIN_LON - 1
    columns = jnp.arange(position_bias.shape[1], dtype=jnp.int32)[:, None, None]
    one_hot = (columns == level_col[None]) | (columns == lat_col[None]) | (columns == lon_col[None])
    one_hot = one_hot.astype(jnp.float32).reshape(position_bias.shape[1], window_size * window_size)
    table = jnp.dot(position_bias, one_hot, precision=lax.Precision.HIGHEST)
    return table.reshape(position_bias.shape[0], window_size, window_size)

def to_windows(grid):
    levels, lat_rows, lon_cols, chans = grid.shape
    blocks = grid.reshape(levels // WIN_LEV, WIN_LEV, lat_rows // WIN_LAT, WIN_LAT, lon_cols // WIN_LON, WIN_LON, chans)
    return blocks.transpose(0, 2, 4, 1, 3, 5, 6).reshape(-1, WIN_LEV * WIN_LAT * WIN_LON, chans)

def from_windows(windows, levels, lat_rows, lon_cols):
    chans = windows.shape[-1]
    blocks = windows.reshape(levels // WIN_LEV, lat_rows // WIN_LAT, lon_cols // WIN_LON, WIN_LEV, WIN_LAT, WIN_LON, chans)
    return blocks.transpose(0, 3, 1, 4, 2, 5, 6).reshape(levels, lat_rows, lon_cols, chans)

def window_pass(x_block, g_block, id_block, bias_table, norm_gain, w_qkv, qkv_down, qkv_up, w_proj, proj_down, proj_up):
    windows, window_size, width = x_block.shape
    rows_total = windows * window_size
    head_size = width // HEADS
    score_scale = 1.0 / math.sqrt(head_size)
    flat_rows = widen(x_block.reshape(rows_total, width))
    average = lax.optimization_barrier(jnp.mean(flat_rows, axis=-1, keepdims=True))
    centered = flat_rows - average
    variance = lax.optimization_barrier(jnp.mean(centered * centered, axis=-1, keepdims=True))
    inv_std = lax.rsqrt(variance + epsilon)
    unit_rows = centered * inv_std
    normed = (unit_rows * norm_gain).astype(jnp.bfloat16)
    low_qkv = dot_rows(normed, qkv_down).astype(jnp.bfloat16)
    qkv = (jnp.dot(widen(normed), w_qkv) + jnp.dot(widen(low_qkv), widen(qkv_up))).astype(jnp.bfloat16)
    pieces = qkv.reshape(windows, window_size, 3, HEADS, head_size)
    query, keys, values = (pieces[:, :, 0], pieces[:, :, 1], pieces[:, :, 2])
    allowed = id_block[:, None, :, None] == id_block[:, None, None, :]
    scores = jnp.einsum('bqhd,bkhd->bhqk', widen(query), widen(keys)) * score_scale + bias_table[None]
    scores = jnp.where(allowed, scores, masked_value)
    row_max = lax.optimization_barrier(jnp.max(scores, axis=-1, keepdims=True))
    exp_terms = jnp.where(allowed, jnp.exp(scores - row_max), 0.0)
    probs_full = exp_terms / lax.optimization_barrier(jnp.sum(exp_terms, axis=-1, keepdims=True))
    probs = probs_full.astype(jnp.bfloat16)
    attn = jnp.einsum('bhqk,bkhd->bqhd', widen(probs), widen(values)).astype(jnp.bfloat16).reshape(rows_total, width)
    low_proj = dot_rows(attn, proj_down).astype(jnp.bfloat16)
    out_rows = (flat_rows + jnp.dot(widen(attn), widen(w_proj)) + jnp.dot(widen(low_proj), widen(proj_up))).astype(jnp.bfloat16)
    grad_rows = g_block.reshape(rows_total, width)
    proj_up_raw = dot_cols(low_proj, grad_rows)
    d_low_proj = dot_rows(grad_rows, proj_up).astype(jnp.bfloat16)
    proj_down_raw = dot_cols(d_low_proj, attn)
    d_attn = (dot_rows(grad_rows, w_proj) + jnp.dot(widen(d_low_proj), widen(proj_down))).astype(jnp.bfloat16)
    d_heads = d_attn.reshape(windows, window_size, HEADS, head_size)
    d_probs = jnp.einsum('bqhd,bkhd->bhqk', widen(d_heads), widen(values))
    d_values = jnp.einsum('bhqk,bqhd->bkhd', widen(probs), widen(d_heads))
    d_scores = (probs_full * (d_probs - lax.optimization_barrier(jnp.sum(d_probs * probs_full, axis=-1, keepdims=True))) * score_scale).astype(jnp.bfloat16)
    d_query = jnp.einsum('bhqk,bkhd->bqhd', widen(d_scores), widen(keys))
    d_keys = jnp.einsum('bhqk,bqhd->bkhd', widen(d_scores), widen(query))
    d_qkv = jnp.stack([d_query, d_keys, d_values], axis=2).astype(jnp.bfloat16).reshape(rows_total, 3 * width)
    qkv_up_raw = dot_cols(low_qkv, d_qkv)
    d_low_qkv = dot_rows(d_qkv, qkv_up).astype(jnp.bfloat16)
    qkv_down_raw = dot_cols(d_low_qkv, normed)
    d_normed = dot_rows(d_qkv, w_qkv) + jnp.dot(widen(d_low_qkv), widen(qkv_down))
    d_unit = d_normed * norm_gain
    norm_back = inv_std * (d_unit - lax.optimization_barrier(jnp.mean(d_unit, axis=-1, keepdims=True)) - unit_rows * lax.optimization_barrier(jnp.mean(d_unit * unit_rows, axis=-1, keepdims=True)))
    grad_in = (widen(grad_rows) + norm_back).astype(jnp.bfloat16)
    return (out_rows.reshape(x_block.shape), grad_in.reshape(x_block.shape), (qkv_down_raw, qkv_up_raw, proj_down_raw, proj_up_raw))

def reference(latent, cotangent, mask_ids, position_bias, norm_gain, w_qkv, qkv_down, qkv_up, w_proj, proj_down, proj_up):
    offsets = (-(WIN_LEV // 2), -(WIN_LAT // 2), -(WIN_LON // 2))
    backs = (WIN_LEV // 2, WIN_LAT // 2, WIN_LON // 2)
    shifted = jnp.roll(latent, offsets, axis=(0, 1, 2))
    grad_shifted = jnp.roll(cotangent, offsets, axis=(0, 1, 2))
    bias_table = window_bias(position_bias)
    wide_qkv = widen(w_qkv)
    window_size = WIN_LEV * WIN_LAT * WIN_LON
    x_windows = to_windows(shifted).reshape(-1, 8, window_size, D)
    g_windows = to_windows(grad_shifted).reshape(-1, 8, window_size, D)
    id_windows = to_windows(mask_ids[..., None])[..., 0].reshape(-1, 8, window_size)

    def block_step(totals, block):
        x_block, g_block, id_block = block
        out_block, grad_block, terms = window_pass(x_block, g_block, id_block, bias_table, norm_gain, wide_qkv, qkv_down, qkv_up, w_proj, proj_down, proj_up)
        return (tuple((total + term for total, term in zip(totals, terms))), (out_block, grad_block))
    initial = (jnp.zeros((RANK, D), jnp.float32), jnp.zeros((RANK, 3 * D), jnp.float32), jnp.zeros((RANK, D), jnp.float32), jnp.zeros((RANK, D), jnp.float32))
    totals, (out_blocks, grad_blocks) = lax.scan(block_step, initial, (x_windows, g_windows, id_windows))
    shifted_out = from_windows(out_blocks.reshape(-1, window_size, D), LEVELS, LAT, LON)
    grad_in = from_windows(grad_blocks.reshape(-1, window_size, D), LEVELS, LAT, LON)
    output = jnp.roll(shifted_out, backs, axis=(0, 1, 2))
    latent_grad = jnp.roll(grad_in, backs, axis=(0, 1, 2))
    grad_scale = 1.0 / math.sqrt(TOKENS)
    return (output, latent_grad, totals[0] * grad_scale, totals[1] * grad_scale, totals[2] * grad_scale, totals[3] * grad_scale)
```

```python
import functools
import math

import jax
import jax.numpy as jnp
import numpy as np
from jax import lax
from jax.experimental import pallas as pl
from jax.experimental.pallas import tpu as pltpu
from jax.sharding import PartitionSpec as P

HEADS = 8
WIN_LEV = 2
WIN_LAT = 6
WIN_LON = 12
REGIONS = 2
PLACES = WIN_LEV + WIN_LAT + WIN_LON

epsilon = 1e-05
barred = -1e30
MESH = pl.DeviceIdType.MESH
f32 = jnp.float32
bf16 = jnp.bfloat16


def mm(a, b):
    return jnp.dot(a, b, preferred_element_type=f32)


def mm_rows(a, b):
    return lax.dot_general(a, b, (((1,), (1,)), ((), ())), preferred_element_type=f32)


def mm_cols(a, b):
    return lax.dot_general(a, b, (((0,), (0,)), ((), ())), preferred_element_type=f32)


def kernel(n_lat, n_lon, reduce_here, grad_scale, *refs):
    (xq, gq, feat, table, gain, w_qkv, qkv_down, qkv_up, w_proj, proj_down, proj_up) = refs[:11]
    (out_o, grad_o, qd_o, qu_o, pd_o, pu_o) = refs[11:17]
    (x_in, g_in, xf, gf, normed_s, qkv_s, kf_s, attn_s, da_s, dqkv_s, probs_s) = refs[17:28]
    (o_send, b_send, o_in, b_in, terms, slots, total) = refs[28:35]
    (in_send, in_recv, out_send, out_recv, rs_send, rs_recv, ag_send, ag_recv) = refs[35:]

    lat, lon = lax.axis_index("lat"), lax.axis_index("lon")
    n = n_lat * n_lon
    me = lat * n_lon + lon

    def near(dlat, dlon):
        return {
            "lat": lax.rem(lat + dlat + n_lat, n_lat),
            "lon": lax.rem(lon + dlon + n_lon, n_lon),
        }

    def far(step):
        other = lax.rem(me + step, n)
        return other, {"lat": other // n_lon, "lon": lax.rem(other, n_lon)}

    barrier = pltpu.get_barrier_semaphore()
    if reduce_here:
        for step in range(1, n):
            pl.semaphore_signal(barrier, inc=1, device_id=far(step)[1], device_id_type=MESH)
        pl.semaphore_wait(barrier, n - 1)
    else:
        for dlat, dlon in ((0, 1), (1, 0), (1, 1)):
            for sign in (1, -1):
                pl.semaphore_signal(
                    barrier, inc=1, device_id=near(sign * dlat, sign * dlon), device_id_type=MESH
                )
        pl.semaphore_wait(barrier, 6)

    moves = []
    for kind, (src, dst) in enumerate(((xq, x_in), (gq, g_in))):
        row = []
        for quarter in (0, 1, 2):
            copy = pltpu.make_async_remote_copy(
                src_ref=src.at[quarter],
                dst_ref=dst.at[quarter],
                send_sem=in_send.at[kind, quarter],
                recv_sem=in_recv.at[kind, quarter],
                device_id=near(-1 if quarter // 2 == 0 else 0, -1 if quarter % 2 == 0 else 0),
                device_id_type=MESH,
            )
            copy.start()
            row.append(copy)
        moves.append(row)

    part = xq.shape[1]
    rows = 4 * part
    width = xq.shape[2]
    pairs = HEADS // 2
    score_scale = 1.0 / math.sqrt(width // HEADS)

    kf_s[...] = mm(feat[...], table[...]).astype(bf16)

    xf[0:part, :] = xq[3].astype(f32)
    gf[0:part, :] = gq[3].astype(f32)
    for quarter in (0, 1, 2):
        moves[0][quarter].wait()
        start = (3 - quarter) * part
        xf[start : start + part, :] = x_in[quarter].astype(f32)

    def norm():
        x = xf[...]
        centered = x - jnp.mean(x, axis=-1, keepdims=True)
        variance = jnp.mean(centered * centered, axis=-1, keepdims=True)
        inv_std = lax.rsqrt(variance + epsilon)
        return centered * inv_std, inv_std

    normed = (norm()[0] * gain[...]).astype(bf16)
    normed_s[...] = normed
    low_qkv = mm_rows(normed, qkv_down[...]).astype(bf16)
    qkv_s[...] = (mm(normed, w_qkv[...]) + mm(low_qkv, qkv_up[...])).astype(bf16)

    left = lax.broadcasted_iota(jnp.int32, (rows, 128), 1) < 64

    def pick(a, b):
        return jnp.where(left, a, b)

    def lanes(first, pair):
        return pl.ds(first + pair * 128, 128)

    def forward_pair(pair):
        query = (qkv_s[:, lanes(0, pair)].astype(f32) * score_scale)
        keys = qkv_s[:, lanes(width, pair)].astype(f32)
        values = qkv_s[:, lanes(2 * width, pair)]
        spots = feat[...].astype(f32)
        offsets = kf_s[:, lanes(0, pair)].astype(f32)
        results = []
        for half in range(2):
            if half == 0:
                q_aug, k_aug = pick(query, spots), pick(keys, offsets)
            else:
                q_aug, k_aug = pick(spots, query), pick(offsets, keys)
            scores = mm_rows(q_aug.astype(bf16), k_aug.astype(bf16))
            terms_e = jnp.exp(scores - jnp.max(scores, axis=-1, keepdims=True))
            probs = terms_e / jnp.sum(terms_e, axis=-1, keepdims=True)
            probs_s[2 * pair + half] = probs
            results.append(mm(probs.astype(bf16), values))
        attn_s[:, lanes(0, pair)] = pick(results[0], results[1]).astype(bf16)

    for pair in range(pairs):
        forward_pair(pair)

    attn = attn_s[...]
    low_proj = mm_rows(attn, proj_down[...]).astype(bf16)
    out_rows = xf[...] + mm(attn, w_proj[...]) + mm(low_proj, proj_up[...])
    for region in range(4):
        slab = out_rows[region * part : (region + 1) * part].astype(bf16)
        if region == 0:
            out_o[3] = slab
        else:
            o_send[3 - region] = slab

    def send_out(kind, src, dst):
        row = []
        for quarter in (0, 1, 2):
            copy = pltpu.make_async_remote_copy(
                src_ref=src.at[quarter],
                dst_ref=dst.at[quarter],
                send_sem=out_send.at[kind, quarter],
                recv_sem=out_recv.at[kind, quarter],
                device_id=near(1 if quarter // 2 == 0 else 0, 1 if quarter % 2 == 0 else 0),
                device_id_type=MESH,
            )
            copy.start()
            row.append(copy)
        return row

    out_moves = send_out(0, o_send, o_in)

    for quarter in (0, 1, 2):
        moves[1][quarter].wait()
        start = (3 - quarter) * part
        gf[start : start + part, :] = g_in[quarter].astype(f32)
    grad_rows = gf[...].astype(bf16)
    proj_up_raw = mm_cols(low_proj, grad_rows)
    d_low_proj = mm_rows(grad_rows, proj_up[...]).astype(bf16)
    proj_down_raw = mm_cols(d_low_proj, attn)
    da_s[...] = (mm_rows(grad_rows, w_proj[...]) + mm(d_low_proj, proj_down[...])).astype(bf16)

    def backward_pair(pair):
        query = qkv_s[:, lanes(0, pair)]
        keys = qkv_s[:, lanes(width, pair)]
        values = qkv_s[:, lanes(2 * width, pair)]
        d_attn = da_s[:, lanes(0, pair)]
        d_attn32 = d_attn.astype(f32)
        d_q, d_k, d_v = [], [], []
        for half in range(2):
            own = pick(d_attn32, 0.0) if half == 0 else pick(0.0, d_attn32)
            probs = probs_s[2 * pair + half]
            d_probs = mm_rows(own.astype(bf16), values)
            inner = jnp.sum(d_probs * probs, axis=-1, keepdims=True)
            d_scores = (probs * (d_probs - inner) * score_scale).astype(bf16)
            d_v.append(mm_cols(probs.astype(bf16), d_attn))
            d_q.append(mm(d_scores, keys))
            d_k.append(mm_cols(d_scores, query))
        dqkv_s[:, lanes(0, pair)] = pick(d_q[0], d_q[1]).astype(bf16)
        dqkv_s[:, lanes(width, pair)] = pick(d_k[0], d_k[1]).astype(bf16)
        dqkv_s[:, lanes(2 * width, pair)] = pick(d_v[0], d_v[1]).astype(bf16)

    for pair in range(pairs):
        backward_pair(pair)

    d_qkv = dqkv_s[...]
    qkv_up_raw = mm_cols(low_qkv, d_qkv)
    d_low_qkv = mm_rows(d_qkv, qkv_up[...]).astype(bf16)
    qkv_down_raw = mm_cols(d_low_qkv, normed_s[...])

    raws = ((qkv_down_raw, qd_o), (qkv_up_raw, qu_o), (proj_down_raw, pd_o), (proj_up_raw, pu_o))
    own_blocks = 0
    places = []
    if reduce_here:
        for raw, out in raws:
            for top in range(0, raw.shape[0], 8):
                for start in range(0, raw.shape[1], 128):
                    terms[len(places)] = raw[top : top + 8, start : start + 128]
                    places.append((out, top, start))
        own_blocks = len(places) // n
        scatter = []
        for step in range(1, n):
            other, where = far(step)
            copy = pltpu.make_async_remote_copy(
                src_ref=terms.at[pl.ds(other * own_blocks, own_blocks)],
                dst_ref=slots.at[step - 1],
                send_sem=rs_send.at[step - 1],
                recv_sem=rs_recv.at[step - 1],
                device_id=where,
                device_id_type=MESH,
            )
            copy.start()
            scatter.append(copy)
    else:
        for raw, out in raws:
            out[...] = raw * grad_scale

    d_normed = mm_rows(d_qkv, w_qkv[...]) + mm(d_low_qkv, qkv_down[...])
    d_unit = d_normed * gain[...]
    unit_rows, inv_std = norm()
    back = inv_std * (
        d_unit
        - jnp.mean(d_unit, axis=-1, keepdims=True)
        - unit_rows * jnp.mean(d_unit * unit_rows, axis=-1, keepdims=True)
    )
    grad_in = gf[...] + back
    for region in range(4):
        slab = grad_in[region * part : (region + 1) * part].astype(bf16)
        if region == 0:
            grad_o[3] = slab
        else:
            b_send[3 - region] = slab
    back_moves = send_out(1, b_send, b_in)

    if reduce_here:
        for copy in scatter:
            copy.wait()
        mine = pl.ds(me * own_blocks, own_blocks)
        acc = terms[mine]
        for step in range(1, n):
            acc = acc + slots[step - 1]
        total[mine] = acc * grad_scale
        gather = []
        for step in range(1, n):
            copy = pltpu.make_async_remote_copy(
                src_ref=total.at[mine],
                dst_ref=total.at[mine],
                send_sem=ag_send.at[step - 1],
                recv_sem=ag_recv.at[step - 1],
                device_id=far(step)[1],
                device_id_type=MESH,
            )
            copy.start()
            gather.append(copy)

    for quarter in (0, 1, 2):
        out_moves[quarter].wait()
        out_o[quarter] = o_in[quarter]
    for quarter in (0, 1, 2):
        back_moves[quarter].wait()
        grad_o[quarter] = b_in[quarter]

    if reduce_here:
        for step, copy in enumerate(gather, 1):
            copy.wait()
        for place, (out, top, start) in enumerate(places):
            out[top : top + 8, start : start + 128] = total[place]


def to_quarters(grid):
    levels, lat_rows, lon_cols = grid.shape[:3]
    rest = grid.shape[3:]
    blocks = grid.reshape((levels, 2, lat_rows // 2, 2, lon_cols // 2) + rest)
    order = (1, 3, 0, 2, 4) + tuple(range(5, 5 + len(rest)))
    return blocks.transpose(order).reshape((4, levels * lat_rows * lon_cols // 4) + rest)


def from_quarters(quarters, levels, lat_rows, lon_cols):
    width = quarters.shape[-1]
    blocks = quarters.reshape(2, 2, levels, lat_rows // 2, lon_cols // 2, width)
    return blocks.transpose(2, 0, 3, 1, 4, 5).reshape(levels, lat_rows, lon_cols, width)


def position_features(mask_ids):
    levels, lat_rows, lon_cols = mask_ids.shape
    grid = np.indices((2, 2, levels, lat_rows // 2, lon_cols // 2)).reshape(5, -1)
    turned = (grid[2] - WIN_LEV // 2) % levels
    lat_pos = grid[0] * (lat_rows // 2) + grid[3]
    lon_pos = grid[1] * (lon_cols // 2) + grid[4]
    spots = np.zeros((grid.shape[1], PLACES), np.float32)
    each = np.arange(grid.shape[1])
    spots[each, turned % WIN_LEV] = 1
    spots[each, WIN_LEV + lat_pos] = 1
    spots[each, WIN_LEV + WIN_LAT + lon_pos] = 1
    groups = levels // WIN_LEV * REGIONS
    ids = to_quarters(jnp.roll(mask_ids, WIN_LEV // 2, axis=0)).reshape(-1)
    ids = ids + jnp.asarray(turned // WIN_LEV * REGIONS, jnp.int32)
    group = (ids[:, None] == jnp.arange(groups, dtype=jnp.int32)).astype(bf16)
    spots = jnp.asarray(spots, bf16)
    once = jnp.concatenate((spots, spots, spots, group), 1)
    return jnp.concatenate((once, once), 1), groups


def offset_table(position_bias, groups):
    heads, columns = position_bias.shape
    place = np.arange(PLACES)
    axis = np.where(place < WIN_LEV, 0, np.where(place < WIN_LEV + WIN_LAT, 1, 2))
    first = np.array([0, WIN_LEV, WIN_LEV + WIN_LAT])[axis]
    pos = place - first
    zero = np.array(
        [WIN_LEV - 1, 2 * WIN_LEV - 1 + WIN_LAT - 1, 2 * WIN_LEV + 2 * WIN_LAT - 2 + WIN_LON - 1]
    )[axis]
    col = zero[:, None] + pos[None, :] - pos[:, None]
    same = axis[:, None] == axis[None, :]
    hot = (np.arange(columns)[:, None, None] == col[None]) & same[None]
    hot = jnp.asarray(hot.reshape(columns, PLACES * PLACES), bf16)
    high = lax.reduce_precision(position_bias, 8, 7)
    rest = position_bias - high
    middle = lax.reduce_precision(rest, 8, 7)
    low = rest - middle
    parts = jnp.stack((high, middle, low)).astype(bf16).reshape(3 * heads, columns)
    picked = mm(parts, hot).astype(bf16).reshape(3, heads, PLACES, PLACES)
    picked = picked.transpose(2, 1, 0, 3).reshape(PLACES, heads, 3 * PLACES)
    picked = jnp.pad(picked, ((0, 0), (0, 0), (0, groups)))
    walls = np.zeros((groups, heads, 3 * PLACES + groups), np.float32)
    walls[:, :, 3 * PLACES :] = (barred * (1 - np.eye(groups)))[:, None, :]
    depth = 3 * PLACES + groups
    full = jnp.concatenate(
        (
            picked,
            jnp.zeros((2 * PLACES, heads, depth), bf16),
            jnp.asarray(walls, bf16),
            jnp.zeros((depth, heads, depth), bf16),
        ),
        0,
    )
    full = full.reshape(2 * depth, heads // 2, 2, depth)[:, :, ::-1]
    return full.reshape(2 * depth, heads * depth)


def on_device(
    n_lat,
    n_lon,
    latent,
    cotangent,
    mask_ids,
    position_bias,
    norm_gain,
    w_qkv,
    qkv_down,
    qkv_up,
    w_proj,
    proj_down,
    proj_up,
):
    levels, lat_rows, lon_cols, width = latent.shape
    assert lat_rows == WIN_LAT and lon_cols == WIN_LON
    rows = levels * lat_rows * lon_cols
    part = rows // 4
    rank = qkv_down.shape[0]
    n = n_lat * n_lon
    feat, groups = position_features(mask_ids)
    table = offset_table(position_bias, groups)
    blocks = rank // 8 * (6 * width // 128)
    reduce_here = blocks % n == 0
    own = blocks // n if reduce_here else 1
    peers = n - 1 if reduce_here else 1
    grad_scale = 1.0 / math.sqrt(rows * n)
    quarter_shape = jax.ShapeDtypeStruct((4, part, width), bf16)
    dma = pltpu.SemaphoreType.DMA
    results = pl.pallas_call(
        functools.partial(kernel, n_lat, n_lon, reduce_here, grad_scale),
        out_shape=(
            quarter_shape,
            quarter_shape,
            jax.ShapeDtypeStruct((rank, width), f32),
            jax.ShapeDtypeStruct((rank, 3 * width), f32),
            jax.ShapeDtypeStruct((rank, width), f32),
            jax.ShapeDtypeStruct((rank, width), f32),
        ),
        in_specs=[pl.BlockSpec(memory_space=pltpu.VMEM)] * 11,
        out_specs=[pl.BlockSpec(memory_space=pltpu.VMEM)] * 6,
        scratch_shapes=[
            pltpu.VMEM((3, part, width), bf16),
            pltpu.VMEM((3, part, width), bf16),
            pltpu.VMEM((rows, width), f32),
            pltpu.VMEM((rows, width), f32),
            pltpu.VMEM((rows, width), bf16),
            pltpu.VMEM((rows, 3 * width), bf16),
            pltpu.VMEM((rows, width), bf16),
            pltpu.VMEM((rows, width), bf16),
            pltpu.VMEM((rows, width), bf16),
            pltpu.VMEM((rows, 3 * width), bf16),
            pltpu.VMEM((HEADS, rows, rows), f32),
            pltpu.VMEM((3, part, width), bf16),
            pltpu.VMEM((3, part, width), bf16),
            pltpu.VMEM((3, part, width), bf16),
            pltpu.VMEM((3, part, width), bf16),
            pltpu.VMEM((blocks, 8, 128), f32),
            pltpu.VMEM((peers, own, 8, 128), f32),
            pltpu.VMEM((blocks, 8, 128), f32),
            dma((2, 3)),
            dma((2, 3)),
            dma((2, 3)),
            dma((2, 3)),
            dma((peers,)),
            dma((peers,)),
            dma((peers,)),
            dma((peers,)),
        ],
        compiler_params=pltpu.CompilerParams(
            collective_id=0, has_side_effects=True, vmem_limit_bytes=60 * 2**20
        ),
        name="sublayer",
    )(
        to_quarters(latent),
        to_quarters(cotangent),
        feat,
        table,
        norm_gain.reshape(1, width),
        w_qkv,
        qkv_down,
        qkv_up,
        w_proj,
        proj_down,
        proj_up,
    )
    output = from_quarters(results[0], levels, lat_rows, lon_cols)
    latent_grad = from_quarters(results[1], levels, lat_rows, lon_cols)
    grads = results[2:]
    if not reduce_here:
        grads = lax.psum(tuple(grads), ("lon", "lat"))
    return (output, latent_grad, *grads)


def solution(mesh):
    return jax.shard_map(
        functools.partial(on_device, mesh.shape["lat"], mesh.shape["lon"]),
        mesh=mesh,
        in_specs=(
            P("runs", "lat", "lon", None),
            P("runs", "lat", "lon", None),
            P("runs", "lat", "lon"),
            P(),
            P(),
            P(),
            P(),
            P(),
            P(),
            P(),
            P(),
        ),
        out_specs=(
            P("runs", "lat", "lon", None),
            P("runs", "lat", "lon", None),
            P("runs", None),
            P("runs", None),
            P("runs", None),
            P("runs", None),
        ),
        check_vma=False,
    )
```

```python
import functools
import math

import jax
import jax.numpy as jnp
import numpy as np
from jax import lax
from jax.experimental import pallas as pl
from jax.experimental.pallas import tpu as pltpu
from jax.sharding import PartitionSpec as P

HEADS = 8
WIN_LEV = 2
WIN_LAT = 6
WIN_LON = 12
REGIONS = 2
PLACES = WIN_LEV + WIN_LAT + WIN_LON
SPOT = WIN_LEV + WIN_LAT

epsilon = 1e-05
barred = -1e30
MESH = pl.DeviceIdType.MESH
f32 = jnp.float32
bf16 = jnp.bfloat16


def mm(a, b):
    return jnp.dot(a, b, preferred_element_type=f32)


def mm_rows(a, b):
    return lax.dot_general(a, b, (((1,), (1,)), ((), ())), preferred_element_type=f32)


def mm_cols(a, b):
    return lax.dot_general(a, b, (((0,), (0,)), ((), ())), preferred_element_type=f32)


def kernel(n_lat, n_lon, reduce_here, grad_scale, *refs):
    (latent, cotangent, mask_ids, position_bias) = refs[:4]
    (base, picker, chosen, columns, walls) = refs[4:9]
    (gain, w_qkv, qkv_down, qkv_up, w_proj, proj_down, proj_up) = refs[9:16]
    (out_o, grad_o, qd_o, qu_o, pd_o, pu_o) = refs[16:22]
    (xq, gq, x_in, g_in, xf, gf, normed_s, qkv_s, kf_s, attn_s, da_s, dqkv_s, probs_s) = refs[22:35]
    (o_send, b_send, o_in, b_in, terms, slots, total) = refs[35:42]
    (feat, table, ids_s, grid_s, hold) = refs[42:47]
    (in_send, in_recv, out_send, out_recv, rs_send, rs_recv, ag_send, ag_recv) = refs[47:]

    lat, lon = lax.axis_index("lat"), lax.axis_index("lon")
    n = n_lat * n_lon
    me = lat * n_lon + lon

    def near(dlat, dlon):
        return {
            "lat": lax.rem(lat + dlat + n_lat, n_lat),
            "lon": lax.rem(lon + dlon + n_lon, n_lon),
        }

    def far(step):
        other = lax.rem(me + step, n)
        return other, {"lat": other // n_lon, "lon": lax.rem(other, n_lon)}

    levels, lat_rows, lon_cols, width = latent.shape
    half_rows, half_cols = lat_rows // 2, lon_cols // 2
    part = xq.shape[1]
    rows = 4 * part
    pairs = HEADS // 2
    score_scale = 1.0 / math.sqrt(width // HEADS)

    barrier = pltpu.get_barrier_semaphore()
    if reduce_here:
        for step in range(1, n):
            pl.semaphore_signal(barrier, inc=1, device_id=far(step)[1], device_id_type=MESH)
    else:
        for dlat, dlon in ((0, 1), (1, 0), (1, 1)):
            for sign in (1, -1):
                pl.semaphore_signal(
                    barrier, inc=1, device_id=near(sign * dlat, sign * dlon), device_id_type=MESH
                )

    def split(grid, flat, quarters):
        for level in range(levels):
            for row in range(lat_rows):
                line = grid[level, row].astype(f32)
                for half in range(2):
                    region = 3 - (row // half_rows * 2 + half)
                    start = region * part + (level * half_rows + row % half_rows) * half_cols
                    piece = line[half * half_cols : (half + 1) * half_cols]
                    flat[start : start + half_cols, :] = piece
        for quarter in range(3):
            start = (3 - quarter) * part
            quarters[quarter] = flat[start : start + part, :].astype(bf16)

    split(latent, xf, xq)
    split(cotangent, gf, gq)
    pl.semaphore_wait(barrier, n - 1 if reduce_here else 6)

    moves = []
    for kind, (src, dst) in enumerate(((xq, x_in), (gq, g_in))):
        row = []
        for quarter in (0, 1, 2):
            copy = pltpu.make_async_remote_copy(
                src_ref=src.at[quarter],
                dst_ref=dst.at[quarter],
                send_sem=in_send.at[kind, quarter],
                recv_sem=in_recv.at[kind, quarter],
                device_id=near(-1 if quarter // 2 == 0 else 0, -1 if quarter % 2 == 0 else 0),
                device_id_type=MESH,
            )
            copy.start()
            row.append(copy)
        moves.append(row)

    ids_s[...] = jnp.zeros_like(ids_s)
    for level in range(levels):
        start = level * lat_rows
        ids_s[start : start + lat_rows, SPOT : SPOT + lon_cols] = mask_ids[level].astype(f32)
    start = levels * lat_rows
    ids_s[start : start + 1, SPOT : SPOT + lon_cols] = jnp.ones((1, lon_cols), f32)
    spots_f = base[...].astype(f32)
    group = jnp.sum(mm(picker[...], ids_s[...].astype(bf16)) * spots_f, axis=-1, keepdims=True)
    lane = lax.broadcasted_iota(jnp.int32, (rows, 128), 1)
    lane = jnp.where(lane >= 64, lane - 64, lane) - 3 * PLACES
    feat[...] = jnp.where(lane.astype(f32) == group, 1.0, spots_f).astype(bf16)

    bias = position_bias[...]
    high = bias.astype(bf16).astype(f32)
    middle = (bias - high).astype(bf16).astype(f32)
    low = bias - high - middle
    parts = jnp.concatenate((high, middle, low), 0).astype(bf16)
    spread = mm_cols(parts, chosen[...])
    column = lax.broadcasted_iota(jnp.int32, spread.shape, 0)
    table[...] = walls[...].astype(f32)
    for place in range(PLACES):
        hit = column == columns[place : place + 1, :]
        table[place : place + 1, :] = jnp.sum(jnp.where(hit, spread, 0.0), axis=0, keepdims=True)
    kf_s[...] = mm(feat[...], table[...].astype(bf16)).astype(bf16)

    for quarter in (0, 1, 2):
        moves[0][quarter].wait()
        start = (3 - quarter) * part
        xf[start : start + part, :] = x_in[quarter].astype(f32)

    def norm():
        x = xf[...]
        centered = x - jnp.mean(x, axis=-1, keepdims=True)
        variance = jnp.mean(centered * centered, axis=-1, keepdims=True)
        inv_std = lax.rsqrt(variance + epsilon)
        return centered * inv_std, inv_std

    normed = (norm()[0] * gain[...]).astype(bf16)
    normed_s[...] = normed
    low_qkv = mm_rows(normed, qkv_down[...]).astype(bf16)
    qkv_s[...] = (mm(normed, w_qkv[...]) + mm(low_qkv, qkv_up[...])).astype(bf16)

    left = lax.broadcasted_iota(jnp.int32, (rows, 128), 1) < 64

    def pick(a, b):
        return jnp.where(left, a, b)

    def lanes(first, pair):
        return pl.ds(first + pair * 128, 128)

    def forward_pair(pair):
        query = (qkv_s[:, lanes(0, pair)].astype(f32) * score_scale)
        keys = qkv_s[:, lanes(width, pair)].astype(f32)
        values = qkv_s[:, lanes(2 * width, pair)]
        spots = feat[...].astype(f32)
        offsets = kf_s[:, lanes(0, pair)].astype(f32)
        results = []
        for half in range(2):
            if half == 0:
                q_aug, k_aug = pick(query, spots), pick(keys, offsets)
            else:
                q_aug, k_aug = pick(spots, query), pick(offsets, keys)
            scores = mm_rows(q_aug.astype(bf16), k_aug.astype(bf16))
            terms_e = jnp.exp(scores - jnp.max(scores, axis=-1, keepdims=True))
            probs = terms_e / jnp.sum(terms_e, axis=-1, keepdims=True)
            probs_s[2 * pair + half] = probs
            results.append(mm(probs.astype(bf16), values))
        attn_s[:, lanes(0, pair)] = pick(results[0], results[1]).astype(bf16)

    for pair in range(pairs):
        forward_pair(pair)

    attn = attn_s[...]
    low_proj = mm_rows(attn, proj_down[...]).astype(bf16)
    out_rows = xf[...] + mm(attn, w_proj[...]) + mm(low_proj, proj_up[...])
    for region in range(4):
        slab = out_rows[region * part : (region + 1) * part].astype(bf16)
        if region == 0:
            hold[0] = slab
        else:
            o_send[3 - region] = slab

    def send_out(kind, src, dst):
        row = []
        for quarter in (0, 1, 2):
            copy = pltpu.make_async_remote_copy(
                src_ref=src.at[quarter],
                dst_ref=dst.at[quarter],
                send_sem=out_send.at[kind, quarter],
                recv_sem=out_recv.at[kind, quarter],
                device_id=near(1 if quarter // 2 == 0 else 0, 1 if quarter % 2 == 0 else 0),
                device_id_type=MESH,
            )
            copy.start()
            row.append(copy)
        return row

    out_moves = send_out(0, o_send, o_in)

    for quarter in (0, 1, 2):
        moves[1][quarter].wait()
        start = (3 - quarter) * part
        gf[start : start + part, :] = g_in[quarter].astype(f32)
    grad_rows = gf[...].astype(bf16)
    proj_up_raw = mm_cols(low_proj, grad_rows)
    d_low_proj = mm_rows(grad_rows, proj_up[...]).astype(bf16)
    proj_down_raw = mm_cols(d_low_proj, attn)
    da_s[...] = (mm_rows(grad_rows, w_proj[...]) + mm(d_low_proj, proj_down[...])).astype(bf16)

    def backward_pair(pair):
        query = qkv_s[:, lanes(0, pair)]
        keys = qkv_s[:, lanes(width, pair)]
        values = qkv_s[:, lanes(2 * width, pair)]
        d_attn = da_s[:, lanes(0, pair)]
        d_attn32 = d_attn.astype(f32)
        d_q, d_k, d_v = [], [], []
        for half in range(2):
            own = pick(d_attn32, 0.0) if half == 0 else pick(0.0, d_attn32)
            probs = probs_s[2 * pair + half]
            d_probs = mm_rows(own.astype(bf16), values)
            inner = jnp.sum(d_probs * probs, axis=-1, keepdims=True)
            d_scores = (probs * (d_probs - inner) * score_scale).astype(bf16)
            d_v.append(mm_cols(probs.astype(bf16), d_attn))
            d_q.append(mm(d_scores, keys))
            d_k.append(mm_cols(d_scores, query))
        dqkv_s[:, lanes(0, pair)] = pick(d_q[0], d_q[1]).astype(bf16)
        dqkv_s[:, lanes(width, pair)] = pick(d_k[0], d_k[1]).astype(bf16)
        dqkv_s[:, lanes(2 * width, pair)] = pick(d_v[0], d_v[1]).astype(bf16)

    for pair in range(pairs):
        backward_pair(pair)

    d_qkv = dqkv_s[...]
    qkv_up_raw = mm_cols(low_qkv, d_qkv)
    d_low_qkv = mm_rows(d_qkv, qkv_up[...]).astype(bf16)
    qkv_down_raw = mm_cols(d_low_qkv, normed_s[...])

    raws = ((qkv_down_raw, qd_o), (qkv_up_raw, qu_o), (proj_down_raw, pd_o), (proj_up_raw, pu_o))
    own_blocks = 0
    places = []
    if reduce_here:
        for raw, out in raws:
            for top in range(0, raw.shape[0], 8):
                for start in range(0, raw.shape[1], 128):
                    terms[len(places)] = raw[top : top + 8, start : start + 128]
                    places.append((out, top, start))
        own_blocks = len(places) // n
        scatter = []
        for step in range(1, n):
            other, where = far(step)
            copy = pltpu.make_async_remote_copy(
                src_ref=terms.at[pl.ds(other * own_blocks, own_blocks)],
                dst_ref=slots.at[step - 1],
                send_sem=rs_send.at[step - 1],
                recv_sem=rs_recv.at[step - 1],
                device_id=where,
                device_id_type=MESH,
            )
            copy.start()
            scatter.append(copy)
    else:
        for raw, out in raws:
            out[...] = raw * grad_scale

    d_normed = mm_rows(d_qkv, w_qkv[...]) + mm(d_low_qkv, qkv_down[...])
    d_unit = d_normed * gain[...]
    unit_rows, inv_std = norm()
    back = inv_std * (
        d_unit
        - jnp.mean(d_unit, axis=-1, keepdims=True)
        - unit_rows * jnp.mean(d_unit * unit_rows, axis=-1, keepdims=True)
    )
    grad_in = gf[...] + back
    for region in range(4):
        slab = grad_in[region * part : (region + 1) * part].astype(bf16)
        if region == 0:
            hold[1] = slab
        else:
            b_send[3 - region] = slab
    back_moves = send_out(1, b_send, b_in)

    if reduce_here:
        for copy in scatter:
            copy.wait()
        mine = pl.ds(me * own_blocks, own_blocks)
        acc = terms[mine]
        for step in range(1, n):
            acc = acc + slots[step - 1]
        total[mine] = acc * grad_scale
        gather = []
        for step in range(1, n):
            copy = pltpu.make_async_remote_copy(
                src_ref=total.at[mine],
                dst_ref=total.at[mine],
                send_sem=ag_send.at[step - 1],
                recv_sem=ag_recv.at[step - 1],
                device_id=far(step)[1],
                device_id_type=MESH,
            )
            copy.start()
            gather.append(copy)

    def join(kind, moved, arrived, out):
        for quarter in range(4):
            if quarter < 3:
                moved[quarter].wait()
                slab = arrived[quarter].astype(f32)
            else:
                slab = hold[kind].astype(f32)
            first_row, first_col = quarter // 2 * half_rows, quarter % 2 * half_cols
            for line in range(levels * half_rows):
                grid_s[
                    line // half_rows,
                    first_row + line % half_rows,
                    first_col : first_col + half_cols,
                ] = slab[line * half_cols : (line + 1) * half_cols]
        out[...] = grid_s[...].astype(bf16)

    join(0, out_moves, o_in, out_o)
    join(1, back_moves, b_in, grad_o)

    if reduce_here:
        for step, copy in enumerate(gather, 1):
            copy.wait()
        for place, (out, top, start) in enumerate(places):
            out[top : top + 8, start : start + 128] = total[place]


def finish(*refs):
    half = len(refs) // 2
    for source, target in zip(refs[:half], refs[half:]):
        target[...] = source[...]


def place_tables(levels, lat_rows, lon_cols, columns):
    grid = np.indices((2, 2, levels, lat_rows // 2, lon_cols // 2)).reshape(5, -1)
    rows = grid.shape[1]
    each = np.arange(rows)
    turned = (grid[2] - WIN_LEV // 2) % levels
    lat_pos = grid[0] * (lat_rows // 2) + grid[3]
    lon_pos = grid[1] * (lon_cols // 2) + grid[4]
    groups = levels // WIN_LEV * REGIONS
    depth = 3 * PLACES + groups
    base = np.zeros((rows, 2 * depth), np.float32)
    for start in range(0, 3 * PLACES, PLACES):
        for half in (0, depth):
            base[each, half + start + turned % WIN_LEV] = 1
            base[each, half + start + WIN_LEV + lat_pos] = 1
            base[each, half + start + SPOT + lon_pos] = 1
    picker = np.zeros((rows, levels * lat_rows + 8), np.float32)
    picker[each, turned * lat_rows + lat_pos] = 1
    picker[each, levels * lat_rows] = turned // WIN_LEV * REGIONS

    place = np.arange(PLACES)
    axis = np.where(place < WIN_LEV, 0, np.where(place < SPOT, 1, 2))
    pos = place - np.array([0, WIN_LEV, SPOT])[axis]
    zero = np.array(
        [WIN_LEV - 1, 2 * WIN_LEV - 1 + WIN_LAT - 1, 2 * WIN_LEV + 2 * WIN_LAT - 2 + WIN_LON - 1]
    )[axis]
    col = np.where(axis[:, None] == axis[None], zero[:, None] + pos[None] - pos[:, None], -1)
    lane = np.arange(HEADS * depth)
    head = (lane // depth) ^ 1
    kind = lane % depth // PLACES
    inside = kind < 3
    cols = np.full((PLACES + 4, HEADS * depth), -1, np.int32)
    cols[:PLACES, inside] = col[:, lane[inside] % depth % PLACES]
    chosen = np.zeros((3 * HEADS, HEADS * depth), np.float32)
    chosen[kind[inside] * HEADS + head[inside], lane[inside]] = 1
    walls = np.zeros((2 * depth, HEADS * depth), np.float32)
    for group in range(groups):
        other = ~inside & (lane % depth - 3 * PLACES != group)
        walls[3 * PLACES + group, other] = barred
    return (
        jnp.asarray(base, bf16),
        jnp.asarray(picker, bf16),
        jnp.asarray(chosen, bf16),
        jnp.asarray(cols),
        jnp.asarray(walls, bf16),
    )


def on_device(
    n_lat,
    n_lon,
    latent,
    cotangent,
    mask_ids,
    position_bias,
    norm_gain,
    w_qkv,
    qkv_down,
    qkv_up,
    w_proj,
    proj_down,
    proj_up,
):
    levels, lat_rows, lon_cols, width = latent.shape
    assert lat_rows == WIN_LAT and lon_cols == WIN_LON
    rows = levels * lat_rows * lon_cols
    part = rows // 4
    rank = qkv_down.shape[0]
    n = n_lat * n_lon
    tables = place_tables(levels, lat_rows, lon_cols, position_bias.shape[1])
    blocks = rank // 8 * (6 * width // 128)
    reduce_here = blocks % n == 0
    own = blocks // n if reduce_here else 1
    peers = n - 1 if reduce_here else 1
    grad_scale = 1.0 / math.sqrt(rows * n)
    grid_shape = jax.ShapeDtypeStruct(latent.shape, bf16)
    shapes = (
        grid_shape,
        grid_shape,
        jax.ShapeDtypeStruct((rank, width), f32),
        jax.ShapeDtypeStruct((rank, 3 * width), f32),
        jax.ShapeDtypeStruct((rank, width), f32),
        jax.ShapeDtypeStruct((rank, width), f32),
    )
    in_vmem = pl.BlockSpec(memory_space=pltpu.VMEM)
    dma = pltpu.SemaphoreType.DMA
    results = pl.pallas_call(
        functools.partial(kernel, n_lat, n_lon, reduce_here, grad_scale),
        out_shape=shapes,
        in_specs=[in_vmem] * 16,
        out_specs=[in_vmem] * 6,
        scratch_shapes=[
            pltpu.VMEM((3, part, width), bf16),
            pltpu.VMEM((3, part, width), bf16),
            pltpu.VMEM((3, part, width), bf16),
            pltpu.VMEM((3, part, width), bf16),
            pltpu.VMEM((rows, width), f32),
            pltpu.VMEM((rows, width), f32),
            pltpu.VMEM((rows, width), bf16),
            pltpu.VMEM((rows, 3 * width), bf16),
            pltpu.VMEM((rows, width), bf16),
            pltpu.VMEM((rows, width), bf16),
            pltpu.VMEM((rows, width), bf16),
            pltpu.VMEM((rows, 3 * width), bf16),
            pltpu.VMEM((HEADS, rows, rows), f32),
            pltpu.VMEM((3, part, width), bf16),
            pltpu.VMEM((3, part, width), bf16),
            pltpu.VMEM((3, part, width), bf16),
            pltpu.VMEM((3, part, width), bf16),
            pltpu.VMEM((blocks, 8, 128), f32),
            pltpu.VMEM((peers, own, 8, 128), f32),
            pltpu.VMEM((blocks, 8, 128), f32),
            pltpu.VMEM((rows, 128), bf16),
            pltpu.VMEM((128, HEADS * 64), f32),
            pltpu.VMEM((levels * lat_rows + 8, 128), f32),
            pltpu.VMEM(latent.shape, f32),
            pltpu.VMEM((2, part, width), bf16),
            dma((2, 3)),
            dma((2, 3)),
            dma((2, 3)),
            dma((2, 3)),
            dma((peers,)),
            dma((peers,)),
            dma((peers,)),
            dma((peers,)),
        ],
        compiler_params=pltpu.CompilerParams(
            collective_id=0, has_side_effects=True, vmem_limit_bytes=60 * 2**20
        ),
        name="sublayer",
    )(
        latent,
        cotangent,
        mask_ids,
        position_bias,
        *tables,
        norm_gain.reshape(1, width),
        w_qkv,
        qkv_down,
        qkv_up,
        w_proj,
        proj_down,
        proj_up,
    )
    if not reduce_here:
        grads = lax.psum(tuple(results[2:]), ("lon", "lat"))
        results = (*results[:2], *grads)
    return pl.pallas_call(
        finish,
        out_shape=shapes,
        in_specs=[in_vmem] * 6,
        out_specs=[in_vmem] * 6,
        name="finish",
    )(*results)


def solution(mesh):
    return jax.shard_map(
        functools.partial(on_device, mesh.shape["lat"], mesh.shape["lon"]),
        mesh=mesh,
        in_specs=(
            P("runs", "lat", "lon", None),
            P("runs", "lat", "lon", None),
            P("runs", "lat", "lon"),
            P(),
            P(),
            P(),
            P(),
            P(),
            P(),
            P(),
            P(),
        ),
        out_specs=(
            P("runs", "lat", "lon", None),
            P("runs", "lat", "lon", None),
            P("runs", None),
            P("runs", None),
            P("runs", None),
            P("runs", None),
        ),
        check_vma=False,
    )
```

```python
import functools
import math

import jax
import jax.numpy as jnp
import numpy as np
from jax import lax
from jax.experimental import pallas as pl
from jax.experimental.pallas import tpu as pltpu
from jax.sharding import PartitionSpec as P

HEADS = 8
WIN_LEV = 2
WIN_LAT = 6
WIN_LON = 12
REGIONS = 2
PLACES = WIN_LEV + WIN_LAT + WIN_LON
SPOT = WIN_LEV + WIN_LAT

epsilon = 1e-05
barred = -1e30
MESH = pl.DeviceIdType.MESH
f32 = jnp.float32
bf16 = jnp.bfloat16


def mm(a, b):
    return jnp.dot(a, b, preferred_element_type=f32)


def mm_rows(a, b):
    return lax.dot_general(a, b, (((1,), (1,)), ((), ())), preferred_element_type=f32)


def mm_cols(a, b):
    return lax.dot_general(a, b, (((0,), (0,)), ((), ())), preferred_element_type=f32)


def kernel(n_lat, n_lon, reduce_here, grad_scale, *refs):
    (latent, cotangent, mask_ids, position_bias) = refs[:4]
    (base, picker, chosen, columns, walls) = refs[4:9]
    (gain, w_qkv_far, qkv_down, qkv_up, w_proj_far, proj_down, proj_up) = refs[9:16]
    (out_o, grad_o, qd_o, qu_o, pd_o, pu_o) = refs[16:22]
    (x_own, g_own, x_in, g_in, xf, gf, normed_s, qkv_s, kf_s, attn_s, da_s, dqkv_s, probs_s) = refs[22:35]
    (o_send, b_send, terms, slots, total) = refs[35:40]
    (feat, table, ids_s, w_qkv, w_proj) = refs[40:45]
    (in_send, in_recv, out_send, out_recv, rs_send, rs_recv, ag_send, ag_recv, near_sem) = refs[45:]

    lat, lon = lax.axis_index("lat"), lax.axis_index("lon")
    n = n_lat * n_lon
    me = lat * n_lon + lon

    def near(dlat, dlon):
        return {
            "lat": lax.rem(lat + dlat + n_lat, n_lat),
            "lon": lax.rem(lon + dlon + n_lon, n_lon),
        }

    def far(step):
        other = lax.rem(me + step, n)
        return other, {"lat": other // n_lon, "lon": lax.rem(other, n_lon)}

    lat_rows, lon_cols, levels, width = latent.shape
    half_rows, half_cols = lat_rows // 2, lon_cols // 2
    part = levels * half_rows * half_cols
    rows = 4 * part
    pairs = HEADS // 2
    score_scale = 1.0 / math.sqrt(width // HEADS)

    barrier = pltpu.get_barrier_semaphore()
    if reduce_here:
        for step in range(1, n):
            pl.semaphore_signal(barrier, inc=1, device_id=far(step)[1], device_id_type=MESH)
    else:
        for dlat, dlon in ((0, 1), (1, 0), (1, 1)):
            for sign in (1, -1):
                pl.semaphore_signal(
                    barrier, inc=1, device_id=near(sign * dlat, sign * dlon), device_id_type=MESH
                )

    def corner(grid, quarter):
        return grid.at[
            pl.ds(quarter // 2 * half_rows, half_rows), pl.ds(quarter % 2 * half_cols, half_cols)
        ]

    locals_ = []
    for index, (src, dst) in enumerate(
        (
            (corner(latent, 3), x_own),
            (w_qkv_far, w_qkv),
            (corner(cotangent, 3), g_own),
            (w_proj_far, w_proj),
        )
    ):
        copy = pltpu.make_async_copy(src, dst, near_sem.at[index])
        copy.start()
        locals_.append(copy)

    def unpack(slab, flat, region):
        for row in range(half_rows):
            for col in range(half_cols):
                start = region * part + (row * half_cols + col) * levels
                flat[start : start + levels, :] = slab[row, col].astype(f32)

    pl.semaphore_wait(barrier, n - 1 if reduce_here else 6)

    moves = []
    for kind, (src, dst) in enumerate(((latent, x_in), (cotangent, g_in))):
        row = []
        for quarter in (0, 1, 2):
            copy = pltpu.make_async_remote_copy(
                src_ref=corner(src, quarter),
                dst_ref=dst.at[quarter],
                send_sem=in_send.at[kind, quarter],
                recv_sem=in_recv.at[kind, quarter],
                device_id=near(-1 if quarter // 2 == 0 else 0, -1 if quarter % 2 == 0 else 0),
                device_id_type=MESH,
            )
            copy.start()
            row.append(copy)
        moves.append(row)

    ids_s[...] = jnp.zeros_like(ids_s)
    for row in range(lat_rows):
        start = row * levels
        ids_s[start : start + levels, SPOT : SPOT + lon_cols] = mask_ids[row].astype(f32)
    start = levels * lat_rows
    ids_s[start : start + 1, SPOT : SPOT + lon_cols] = jnp.ones((1, lon_cols), f32)
    spots_f = base[...].astype(f32)
    group = jnp.sum(mm(picker[...], ids_s[...].astype(bf16)) * spots_f, axis=-1, keepdims=True)
    lane = lax.broadcasted_iota(jnp.int32, (rows, 128), 1)
    lane = jnp.where(lane >= 64, lane - 64, lane) - 3 * PLACES
    feat[...] = jnp.where(lane.astype(f32) == group, 1.0, spots_f).astype(bf16)

    bias = position_bias[...]
    high = bias.astype(bf16).astype(f32)
    middle = (bias - high).astype(bf16).astype(f32)
    low = bias - high - middle
    parts = jnp.concatenate((high, middle, low), 0).astype(bf16)
    spread = mm_cols(parts, chosen[...])
    column = lax.broadcasted_iota(jnp.int32, spread.shape, 0)
    table[...] = walls[...].astype(f32)
    for place in range(PLACES):
        hit = column == columns[place : place + 1, :]
        table[place : place + 1, :] = jnp.sum(jnp.where(hit, spread, 0.0), axis=0, keepdims=True)
    kf_s[...] = mm(feat[...], table[...].astype(bf16)).astype(bf16)

    locals_[0].wait()
    unpack(x_own, xf, 0)
    for quarter in (0, 1, 2):
        moves[0][quarter].wait()
        unpack(x_in.at[quarter], xf, 3 - quarter)

    def norm():
        x = xf[...]
        centered = x - jnp.mean(x, axis=-1, keepdims=True)
        variance = jnp.mean(centered * centered, axis=-1, keepdims=True)
        inv_std = lax.rsqrt(variance + epsilon)
        return centered * inv_std, inv_std

    normed = (norm()[0] * gain[...]).astype(bf16)
    normed_s[...] = normed
    low_qkv = mm_rows(normed, qkv_down[...]).astype(bf16)
    locals_[1].wait()
    qkv_s[...] = (mm(normed, w_qkv[...]) + mm(low_qkv, qkv_up[...])).astype(bf16)

    left = lax.broadcasted_iota(jnp.int32, (rows, 128), 1) < 64

    def pick(a, b):
        return jnp.where(left, a, b)

    def lanes(first, pair):
        return pl.ds(first + pair * 128, 128)

    def forward_pair(pair):
        query = (qkv_s[:, lanes(0, pair)].astype(f32) * score_scale)
        keys = qkv_s[:, lanes(width, pair)].astype(f32)
        values = qkv_s[:, lanes(2 * width, pair)]
        spots = feat[...].astype(f32)
        offsets = kf_s[:, lanes(0, pair)].astype(f32)
        results = []
        for half in range(2):
            if half == 0:
                q_aug, k_aug = pick(query, spots), pick(keys, offsets)
            else:
                q_aug, k_aug = pick(spots, query), pick(offsets, keys)
            scores = mm_rows(q_aug.astype(bf16), k_aug.astype(bf16))
            terms_e = jnp.exp(scores - jnp.max(scores, axis=-1, keepdims=True))
            probs = terms_e / jnp.sum(terms_e, axis=-1, keepdims=True)
            probs_s[2 * pair + half] = probs
            results.append(mm(probs.astype(bf16), values))
        attn_s[:, lanes(0, pair)] = pick(results[0], results[1]).astype(bf16)

    for pair in range(pairs):
        forward_pair(pair)

    attn = attn_s[...]
    low_proj = mm_rows(attn, proj_down[...]).astype(bf16)
    locals_[3].wait()
    out_rows = xf[...] + mm(attn, w_proj[...]) + mm(low_proj, proj_up[...])
    def pack(value, region, slab):
        for row in range(half_rows):
            for col in range(half_cols):
                start = region * part + (row * half_cols + col) * levels
                slab[row, col] = value[start : start + levels].astype(bf16)

    for region in (3, 2, 1):
        pack(out_rows, region, o_send.at[3 - region])

    def send_out(kind, src, dst):
        row = []
        for quarter in (0, 1, 2):
            copy = pltpu.make_async_remote_copy(
                src_ref=src.at[quarter],
                dst_ref=corner(dst, quarter),
                send_sem=out_send.at[kind, quarter],
                recv_sem=out_recv.at[kind, quarter],
                device_id=near(1 if quarter // 2 == 0 else 0, 1 if quarter % 2 == 0 else 0),
                device_id_type=MESH,
            )
            copy.start()
            row.append(copy)
        return row

    out_moves = send_out(0, o_send, out_o)
    pack(out_rows, 0, corner(out_o, 3))

    locals_[2].wait()
    unpack(g_own, gf, 0)
    for quarter in (0, 1, 2):
        moves[1][quarter].wait()
        unpack(g_in.at[quarter], gf, 3 - quarter)
    grad_rows = gf[...].astype(bf16)
    proj_up_raw = mm_cols(low_proj, grad_rows)
    d_low_proj = mm_rows(grad_rows, proj_up[...]).astype(bf16)
    proj_down_raw = mm_cols(d_low_proj, attn)
    da_s[...] = (mm_rows(grad_rows, w_proj[...]) + mm(d_low_proj, proj_down[...])).astype(bf16)

    def backward_pair(pair):
        query = qkv_s[:, lanes(0, pair)]
        keys = qkv_s[:, lanes(width, pair)]
        values = qkv_s[:, lanes(2 * width, pair)]
        d_attn = da_s[:, lanes(0, pair)]
        d_attn32 = d_attn.astype(f32)
        d_q, d_k, d_v = [], [], []
        for half in range(2):
            own = pick(d_attn32, 0.0) if half == 0 else pick(0.0, d_attn32)
            probs = probs_s[2 * pair + half]
            d_probs = mm_rows(own.astype(bf16), values)
            inner = jnp.sum(d_probs * probs, axis=-1, keepdims=True)
            d_scores = (probs * (d_probs - inner) * score_scale).astype(bf16)
            d_v.append(mm_cols(probs.astype(bf16), d_attn))
            d_q.append(mm(d_scores, keys))
            d_k.append(mm_cols(d_scores, query))
        dqkv_s[:, lanes(0, pair)] = pick(d_q[0], d_q[1]).astype(bf16)
        dqkv_s[:, lanes(width, pair)] = pick(d_k[0], d_k[1]).astype(bf16)
        dqkv_s[:, lanes(2 * width, pair)] = pick(d_v[0], d_v[1]).astype(bf16)

    for pair in range(pairs):
        backward_pair(pair)

    d_qkv = dqkv_s[...]
    qkv_up_raw = mm_cols(low_qkv, d_qkv)
    d_low_qkv = mm_rows(d_qkv, qkv_up[...]).astype(bf16)
    qkv_down_raw = mm_cols(d_low_qkv, normed_s[...])

    raws = ((qkv_down_raw, qd_o), (qkv_up_raw, qu_o), (proj_down_raw, pd_o), (proj_up_raw, pu_o))
    own_blocks = 0
    places = []
    if reduce_here:
        for raw, out in raws:
            for top in range(0, raw.shape[0], 8):
                for start in range(0, raw.shape[1], 128):
                    terms[len(places)] = raw[top : top + 8, start : start + 128]
                    places.append((out, top, start))
        own_blocks = len(places) // n
        scatter = []
        for step in range(1, n):
            other, where = far(step)
            copy = pltpu.make_async_remote_copy(
                src_ref=terms.at[pl.ds(other * own_blocks, own_blocks)],
                dst_ref=slots.at[step - 1],
                send_sem=rs_send.at[step - 1],
                recv_sem=rs_recv.at[step - 1],
                device_id=where,
                device_id_type=MESH,
            )
            copy.start()
            scatter.append(copy)
    else:
        for raw, out in raws:
            out[...] = raw * grad_scale

    d_normed = mm_rows(d_qkv, w_qkv[...]) + mm(d_low_qkv, qkv_down[...])
    d_unit = d_normed * gain[...]
    unit_rows, inv_std = norm()
    back = inv_std * (
        d_unit
        - jnp.mean(d_unit, axis=-1, keepdims=True)
        - unit_rows * jnp.mean(d_unit * unit_rows, axis=-1, keepdims=True)
    )
    grad_in = gf[...] + back
    for region in (3, 2, 1):
        pack(grad_in, region, b_send.at[3 - region])
    back_moves = send_out(1, b_send, grad_o)
    pack(grad_in, 0, corner(grad_o, 3))

    if reduce_here:
        for copy in scatter:
            copy.wait()
        mine = pl.ds(me * own_blocks, own_blocks)
        acc = terms[mine]
        for step in range(1, n):
            acc = acc + slots[step - 1]
        total[mine] = acc * grad_scale
        gather = []
        for step in range(1, n):
            copy = pltpu.make_async_remote_copy(
                src_ref=total.at[mine],
                dst_ref=total.at[mine],
                send_sem=ag_send.at[step - 1],
                recv_sem=ag_recv.at[step - 1],
                device_id=far(step)[1],
                device_id_type=MESH,
            )
            copy.start()
            gather.append(copy)

    for quarter in (0, 1, 2):
        out_moves[quarter].wait()
        back_moves[quarter].wait()

    if reduce_here:
        for step, copy in enumerate(gather, 1):
            copy.wait()
        for place, (out, top, start) in enumerate(places):
            out[top : top + 8, start : start + 128] = total[place]


def finish(*refs):
    half = len(refs) // 2
    for source, target in zip(refs[:half], refs[half:]):
        target[...] = source[...]


def place_tables(levels, lat_rows, lon_cols, columns):
    grid = np.indices((2, 2, lat_rows // 2, lon_cols // 2, levels)).reshape(5, -1)
    rows = grid.shape[1]
    each = np.arange(rows)
    turned = (grid[4] - WIN_LEV // 2) % levels
    lat_pos = grid[0] * (lat_rows // 2) + grid[2]
    lon_pos = grid[1] * (lon_cols // 2) + grid[3]
    groups = levels // WIN_LEV * REGIONS
    depth = 3 * PLACES + groups
    base = np.zeros((rows, 2 * depth), np.float32)
    for start in range(0, 3 * PLACES, PLACES):
        for half in (0, depth):
            base[each, half + start + turned % WIN_LEV] = 1
            base[each, half + start + WIN_LEV + lat_pos] = 1
            base[each, half + start + SPOT + lon_pos] = 1
    picker = np.zeros((rows, levels * lat_rows + 8), np.float32)
    picker[each, lat_pos * levels + turned] = 1
    picker[each, levels * lat_rows] = turned // WIN_LEV * REGIONS

    place = np.arange(PLACES)
    axis = np.where(place < WIN_LEV, 0, np.where(place < SPOT, 1, 2))
    pos = place - np.array([0, WIN_LEV, SPOT])[axis]
    zero = np.array(
        [WIN_LEV - 1, 2 * WIN_LEV - 1 + WIN_LAT - 1, 2 * WIN_LEV + 2 * WIN_LAT - 2 + WIN_LON - 1]
    )[axis]
    col = np.where(axis[:, None] == axis[None], zero[:, None] + pos[None] - pos[:, None], -1)
    lane = np.arange(HEADS * depth)
    head = (lane // depth) ^ 1
    kind = lane % depth // PLACES
    inside = kind < 3
    cols = np.full((PLACES + 4, HEADS * depth), -1, np.int32)
    cols[:PLACES, inside] = col[:, lane[inside] % depth % PLACES]
    chosen = np.zeros((3 * HEADS, HEADS * depth), np.float32)
    chosen[kind[inside] * HEADS + head[inside], lane[inside]] = 1
    walls = np.zeros((2 * depth, HEADS * depth), np.float32)
    for group in range(groups):
        other = ~inside & (lane % depth - 3 * PLACES != group)
        walls[3 * PLACES + group, other] = barred
    return (
        jnp.asarray(base, bf16),
        jnp.asarray(picker, bf16),
        jnp.asarray(chosen, bf16),
        jnp.asarray(cols),
        jnp.asarray(walls, bf16),
    )


def on_device(
    n_lat,
    n_lon,
    latent,
    cotangent,
    mask_ids,
    position_bias,
    norm_gain,
    w_qkv,
    qkv_down,
    qkv_up,
    w_proj,
    proj_down,
    proj_up,
):
    levels, lat_rows, lon_cols, width = latent.shape
    assert lat_rows == WIN_LAT and lon_cols == WIN_LON
    rows = levels * lat_rows * lon_cols
    part = rows // 4
    rank = qkv_down.shape[0]
    n = n_lat * n_lon
    tables = place_tables(levels, lat_rows, lon_cols, position_bias.shape[1])
    blocks = rank // 8 * (6 * width // 128)
    reduce_here = blocks % n == 0
    own = blocks // n if reduce_here else 1
    peers = n - 1 if reduce_here else 1
    grad_scale = 1.0 / math.sqrt(rows * n)
    grid_shape = jax.ShapeDtypeStruct((lat_rows, lon_cols, levels, width), bf16)
    slab = (lat_rows // 2, lon_cols // 2, levels, width)
    in_place = pl.BlockSpec(memory_space=pl.ANY)
    shapes = (
        grid_shape,
        grid_shape,
        jax.ShapeDtypeStruct((rank, width), f32),
        jax.ShapeDtypeStruct((rank, 3 * width), f32),
        jax.ShapeDtypeStruct((rank, width), f32),
        jax.ShapeDtypeStruct((rank, width), f32),
    )
    in_vmem = pl.BlockSpec(memory_space=pltpu.VMEM)
    dma = pltpu.SemaphoreType.DMA
    results = pl.pallas_call(
        functools.partial(kernel, n_lat, n_lon, reduce_here, grad_scale),
        out_shape=shapes,
        in_specs=[
            in_place if index in (0, 1, 10, 13) else in_vmem for index in range(16)
        ],
        out_specs=[in_vmem] * 6,
        scratch_shapes=[
            pltpu.VMEM(slab, bf16),
            pltpu.VMEM(slab, bf16),
            pltpu.VMEM((3, *slab), bf16),
            pltpu.VMEM((3, *slab), bf16),
            pltpu.VMEM((rows, width), f32),
            pltpu.VMEM((rows, width), f32),
            pltpu.VMEM((rows, width), bf16),
            pltpu.VMEM((rows, 3 * width), bf16),
            pltpu.VMEM((rows, width), bf16),
            pltpu.VMEM((rows, width), bf16),
            pltpu.VMEM((rows, width), bf16),
            pltpu.VMEM((rows, 3 * width), bf16),
            pltpu.VMEM((HEADS, rows, rows), f32),
            pltpu.VMEM((3, *slab), bf16),
            pltpu.VMEM((3, *slab), bf16),
            pltpu.VMEM((blocks, 8, 128), f32),
            pltpu.VMEM((peers, own, 8, 128), f32),
            pltpu.VMEM((blocks, 8, 128), f32),
            pltpu.VMEM((rows, 128), bf16),
            pltpu.VMEM((128, HEADS * 64), f32),
            pltpu.VMEM((levels * lat_rows + 8, 128), f32),
            pltpu.VMEM((width, 3 * width), bf16),
            pltpu.VMEM((width, width), bf16),
            dma((2, 3)),
            dma((2, 3)),
            dma((2, 3)),
            dma((2, 3)),
            dma((peers,)),
            dma((peers,)),
            dma((peers,)),
            dma((peers,)),
            dma((4,)),
        ],
        compiler_params=pltpu.CompilerParams(
            collective_id=0, has_side_effects=True, vmem_limit_bytes=60 * 2**20
        ),
        name="sublayer",
    )(
        latent.transpose(1, 2, 0, 3),
        cotangent.transpose(1, 2, 0, 3),
        mask_ids.transpose(1, 0, 2),
        position_bias,
        *tables,
        norm_gain.reshape(1, width),
        w_qkv,
        qkv_down,
        qkv_up,
        w_proj,
        proj_down,
        proj_up,
    )
    if not reduce_here:
        grads = lax.psum(tuple(results[2:]), ("lon", "lat"))
        results = (*results[:2], *grads)
    output, latent_grad, *grads = pl.pallas_call(
        finish,
        out_shape=shapes,
        in_specs=[in_vmem] * 6,
        out_specs=[in_vmem] * 6,
        name="finish",
    )(*results)
    return (output.transpose(2, 0, 1, 3), latent_grad.transpose(2, 0, 1, 3), *grads)


def solution(mesh):
    return jax.shard_map(
        functools.partial(on_device, mesh.shape["lat"], mesh.shape["lon"]),
        mesh=mesh,
        in_specs=(
            P("runs", "lat", "lon", None),
            P("runs", "lat", "lon", None),
            P("runs", "lat", "lon"),
            P(),
            P(),
            P(),
            P(),
            P(),
            P(),
            P(),
            P(),
        ),
        out_specs=(
            P("runs", "lat", "lon", None),
            P("runs", "lat", "lon", None),
            P("runs", None),
            P("runs", None),
            P("runs", None),
            P("runs", None),
        ),
        check_vma=False,
    )
```

```python
import functools
import math

import jax
import jax.numpy as jnp
import numpy as np
from jax import lax
from jax.experimental import pallas as pl
from jax.experimental.pallas import tpu as pltpu
from jax.sharding import PartitionSpec as P

HEADS = 8
WIN_LEV = 2
WIN_LAT = 6
WIN_LON = 12
REGIONS = 2
PLACES = WIN_LEV + WIN_LAT + WIN_LON
SPOT = WIN_LEV + WIN_LAT

epsilon = 1e-05
barred = -1e30
MESH = pl.DeviceIdType.MESH
f32 = jnp.float32
bf16 = jnp.bfloat16


def mm(a, b):
    return jnp.dot(a, b, preferred_element_type=f32)


def mm_rows(a, b):
    return lax.dot_general(a, b, (((1,), (1,)), ((), ())), preferred_element_type=f32)


def mm_cols(a, b):
    return lax.dot_general(a, b, (((0,), (0,)), ((), ())), preferred_element_type=f32)


def kernel(n_lat, n_lon, reduce_here, grad_scale, *refs):
    (latent, cotangent, mask_ids, position_bias) = refs[:4]
    (base, picker, chosen, columns, walls) = refs[4:9]
    (gain, w_qkv_far, qkv_down, qkv_up, w_proj_far, proj_down, proj_up) = refs[9:16]
    (out_o, grad_o, qd_o, qu_o, pd_o, pu_o) = refs[16:22]
    (x_own, g_own, x_in, g_in, xf, gf, normed_s, qkv_s, kf_s, attn_s, da_s, dqkv_s, probs_s) = refs[22:35]
    (o_send, b_send, terms, slots, total) = refs[35:40]
    (feat, table, ids_s, w_qkv, w_proj) = refs[40:45]
    (in_send, in_recv, out_send, out_recv, rs_send, rs_recv, ag_send, ag_recv, near_sem) = refs[45:]

    lat, lon = lax.axis_index("lat"), lax.axis_index("lon")
    n = n_lat * n_lon
    me = lat * n_lon + lon

    def near(dlat, dlon):
        return {
            "lat": lax.rem(lat + dlat + n_lat, n_lat),
            "lon": lax.rem(lon + dlon + n_lon, n_lon),
        }

    def far(step):
        other = lax.rem(me + step, n)
        return other, {"lat": other // n_lon, "lon": lax.rem(other, n_lon)}

    lat_rows, lon_cols, levels, width = latent.shape
    half_rows, half_cols = lat_rows // 2, lon_cols // 2
    part = levels * half_rows * half_cols
    rows = 4 * part
    pairs = HEADS // 2
    score_scale = 1.0 / math.sqrt(width // HEADS)

    barrier = pltpu.get_barrier_semaphore()
    if reduce_here:
        for step in range(1, n):
            pl.semaphore_signal(barrier, inc=1, device_id=far(step)[1], device_id_type=MESH)
    else:
        for dlat, dlon in ((0, 1), (1, 0), (1, 1)):
            for sign in (1, -1):
                pl.semaphore_signal(
                    barrier, inc=1, device_id=near(sign * dlat, sign * dlon), device_id_type=MESH
                )

    def corner(grid, quarter):
        return grid.at[
            pl.ds(quarter // 2 * half_rows, half_rows), pl.ds(quarter % 2 * half_cols, half_cols)
        ]

    locals_ = []
    for index, (src, dst) in enumerate(
        (
            (corner(latent, 3), x_own),
            (w_qkv_far, w_qkv),
            (corner(cotangent, 3), g_own),
            (w_proj_far, w_proj),
        )
    ):
        copy = pltpu.make_async_copy(src, dst, near_sem.at[index])
        copy.start()
        locals_.append(copy)

    def unpack(slab, flat, region):
        for row in range(half_rows):
            for col in range(half_cols):
                start = region * part + (row * half_cols + col) * levels
                flat[start : start + levels, :] = slab[row, col].astype(f32)

    pl.semaphore_wait(barrier, n - 1 if reduce_here else 6)

    moves = []
    for kind, (src, dst) in enumerate(((latent, x_in), (cotangent, g_in))):
        row = []
        for quarter in (0, 1, 2):
            copy = pltpu.make_async_remote_copy(
                src_ref=corner(src, quarter),
                dst_ref=dst.at[quarter],
                send_sem=in_send.at[kind, quarter],
                recv_sem=in_recv.at[kind, quarter],
                device_id=near(-1 if quarter // 2 == 0 else 0, -1 if quarter % 2 == 0 else 0),
                device_id_type=MESH,
            )
            copy.start()
            row.append(copy)
        moves.append(row)

    ids_s[...] = jnp.zeros_like(ids_s)
    for row in range(lat_rows):
        start = row * levels
        ids_s[start : start + levels, SPOT : SPOT + lon_cols] = mask_ids[row].astype(f32)
    start = levels * lat_rows
    ids_s[start : start + 1, SPOT : SPOT + lon_cols] = jnp.ones((1, lon_cols), f32)
    spots_f = base[...].astype(f32)
    group = jnp.sum(mm(picker[...], ids_s[...].astype(bf16)) * spots_f, axis=-1, keepdims=True)
    lane = lax.broadcasted_iota(jnp.int32, (rows, 128), 1)
    lane = jnp.where(lane >= 64, lane - 64, lane) - 3 * PLACES
    feat[...] = jnp.where(lane.astype(f32) == group, 1.0, spots_f).astype(bf16)

    bias = position_bias[...]
    high = bias.astype(bf16).astype(f32)
    middle = (bias - high).astype(bf16).astype(f32)
    low = bias - high - middle
    parts = jnp.concatenate((high, middle, low), 0).astype(bf16)
    spread = mm_cols(parts, chosen[...])
    column = lax.broadcasted_iota(jnp.int32, spread.shape, 0)
    table[...] = walls[...].astype(f32)
    for place in range(PLACES):
        hit = column == columns[place : place + 1, :]
        table[place : place + 1, :] = jnp.sum(jnp.where(hit, spread, 0.0), axis=0, keepdims=True)
    kf_s[...] = mm(feat[...], table[...].astype(bf16)).astype(bf16)

    locals_[0].wait()
    unpack(x_own, xf, 0)
    for quarter in (0, 1, 2):
        moves[0][quarter].wait()
        unpack(x_in.at[quarter], xf, 3 - quarter)

    def norm():
        x = xf[...]
        centered = x - jnp.mean(x, axis=-1, keepdims=True)
        variance = jnp.mean(centered * centered, axis=-1, keepdims=True)
        inv_std = lax.rsqrt(variance + epsilon)
        return centered * inv_std, inv_std

    normed = (norm()[0] * gain[...]).astype(bf16)
    normed_s[...] = normed
    low_qkv = mm_rows(normed, qkv_down[...]).astype(bf16)
    locals_[1].wait()
    qkv_s[...] = (mm(normed, w_qkv[...]) + mm(low_qkv, qkv_up[...])).astype(bf16)

    left = lax.broadcasted_iota(jnp.int32, (rows, 128), 1) < 64

    def pick(a, b):
        return jnp.where(left, a, b)

    def lanes(first, pair):
        return pl.ds(first + pair * 128, 128)

    def forward_pair(pair):
        query = (qkv_s[:, lanes(0, pair)].astype(f32) * score_scale)
        keys = qkv_s[:, lanes(width, pair)].astype(f32)
        values = qkv_s[:, lanes(2 * width, pair)]
        spots = feat[...].astype(f32)
        offsets = kf_s[:, lanes(0, pair)].astype(f32)
        results = []
        for half in range(2):
            if half == 0:
                q_aug, k_aug = pick(query, spots), pick(keys, offsets)
            else:
                q_aug, k_aug = pick(spots, query), pick(offsets, keys)
            scores = mm_rows(q_aug.astype(bf16), k_aug.astype(bf16))
            terms_e = jnp.exp(scores - jnp.max(scores, axis=-1, keepdims=True))
            probs = terms_e / jnp.sum(terms_e, axis=-1, keepdims=True)
            probs_s[2 * pair + half] = probs
            results.append(mm(probs.astype(bf16), values))
        attn_s[:, lanes(0, pair)] = pick(results[0], results[1]).astype(bf16)

    for pair in range(pairs):
        forward_pair(pair)

    attn = attn_s[...]
    low_proj = mm_rows(attn, proj_down[...]).astype(bf16)
    locals_[3].wait()
    out_rows = xf[...] + mm(attn, w_proj[...]) + mm(low_proj, proj_up[...])
    def pack(value, region, slab):
        for row in range(half_rows):
            for col in range(half_cols):
                start = region * part + (row * half_cols + col) * levels
                slab[row, col] = value[start : start + levels].astype(bf16)

    for region in (3, 2, 1):
        pack(out_rows, region, o_send.at[3 - region])

    def send_out(kind, src, dst):
        row = []
        for quarter in (0, 1, 2):
            copy = pltpu.make_async_remote_copy(
                src_ref=src.at[quarter],
                dst_ref=corner(dst, quarter),
                send_sem=out_send.at[kind, quarter],
                recv_sem=out_recv.at[kind, quarter],
                device_id=near(1 if quarter // 2 == 0 else 0, 1 if quarter % 2 == 0 else 0),
                device_id_type=MESH,
            )
            copy.start()
            row.append(copy)
        return row

    out_moves = send_out(0, o_send, out_o)
    pack(out_rows, 0, corner(out_o, 3))

    locals_[2].wait()
    unpack(g_own, gf, 0)
    for quarter in (0, 1, 2):
        moves[1][quarter].wait()
        unpack(g_in.at[quarter], gf, 3 - quarter)
    grad_rows = gf[...].astype(bf16)
    proj_up_raw = mm_cols(low_proj, grad_rows)
    d_low_proj = mm_rows(grad_rows, proj_up[...]).astype(bf16)
    proj_down_raw = mm_cols(d_low_proj, attn)
    da_s[...] = (mm_rows(grad_rows, w_proj[...]) + mm(d_low_proj, proj_down[...])).astype(bf16)

    def backward_pair(pair):
        query = qkv_s[:, lanes(0, pair)]
        keys = qkv_s[:, lanes(width, pair)]
        values = qkv_s[:, lanes(2 * width, pair)]
        d_attn = da_s[:, lanes(0, pair)]
        d_attn32 = d_attn.astype(f32)
        d_q, d_k, d_v = [], [], []
        for half in range(2):
            own = pick(d_attn32, 0.0) if half == 0 else pick(0.0, d_attn32)
            probs = probs_s[2 * pair + half]
            d_probs = mm_rows(own.astype(bf16), values)
            inner = jnp.sum(d_probs * probs, axis=-1, keepdims=True)
            d_scores = (probs * (d_probs - inner) * score_scale).astype(bf16)
            d_v.append(mm_cols(probs.astype(bf16), d_attn))
            d_q.append(mm(d_scores, keys))
            d_k.append(mm_cols(d_scores, query))
        dqkv_s[:, lanes(0, pair)] = pick(d_q[0], d_q[1]).astype(bf16)
        dqkv_s[:, lanes(width, pair)] = pick(d_k[0], d_k[1]).astype(bf16)
        dqkv_s[:, lanes(2 * width, pair)] = pick(d_v[0], d_v[1]).astype(bf16)

    for pair in range(pairs):
        backward_pair(pair)

    d_qkv = dqkv_s[...]
    qkv_up_raw = mm_cols(low_qkv, d_qkv)
    d_low_qkv = mm_rows(d_qkv, qkv_up[...]).astype(bf16)
    qkv_down_raw = mm_cols(d_low_qkv, normed_s[...])

    raws = ((qkv_down_raw, qd_o), (qkv_up_raw, qu_o), (proj_down_raw, pd_o), (proj_up_raw, pu_o))
    own_blocks = 0
    places = []
    if reduce_here:
        for raw, out in raws:
            for top in range(0, raw.shape[0], 8):
                for start in range(0, raw.shape[1], 128):
                    terms[len(places)] = raw[top : top + 8, start : start + 128].astype(bf16)
                    places.append((out, top, start))
        own_blocks = len(places) // n
        scatter = []
        for step in range(1, n):
            other, where = far(step)
            copy = pltpu.make_async_remote_copy(
                src_ref=terms.at[pl.ds(other * own_blocks, own_blocks)],
                dst_ref=slots.at[step - 1],
                send_sem=rs_send.at[step - 1],
                recv_sem=rs_recv.at[step - 1],
                device_id=where,
                device_id_type=MESH,
            )
            copy.start()
            scatter.append(copy)
    else:
        for raw, out in raws:
            out[...] = raw * grad_scale

    d_normed = mm_rows(d_qkv, w_qkv[...]) + mm(d_low_qkv, qkv_down[...])
    d_unit = d_normed * gain[...]
    unit_rows, inv_std = norm()
    back = inv_std * (
        d_unit
        - jnp.mean(d_unit, axis=-1, keepdims=True)
        - unit_rows * jnp.mean(d_unit * unit_rows, axis=-1, keepdims=True)
    )
    grad_in = gf[...] + back
    for region in (3, 2, 1):
        pack(grad_in, region, b_send.at[3 - region])
    back_moves = send_out(1, b_send, grad_o)
    pack(grad_in, 0, corner(grad_o, 3))

    if reduce_here:
        for copy in scatter:
            copy.wait()
        mine = pl.ds(me * own_blocks, own_blocks)
        acc = terms[mine].astype(f32)
        for step in range(1, n):
            acc = acc + slots[step - 1].astype(f32)
        total[mine] = acc.astype(bf16)
        gather = []
        for step in range(1, n):
            copy = pltpu.make_async_remote_copy(
                src_ref=total.at[mine],
                dst_ref=total.at[mine],
                send_sem=ag_send.at[step - 1],
                recv_sem=ag_recv.at[step - 1],
                device_id=far(step)[1],
                device_id_type=MESH,
            )
            copy.start()
            gather.append(copy)

    for quarter in (0, 1, 2):
        out_moves[quarter].wait()
        back_moves[quarter].wait()

    if reduce_here:
        for step, copy in enumerate(gather, 1):
            copy.wait()
        for place, (out, top, start) in enumerate(places):
            out[top : top + 8, start : start + 128] = total[place].astype(f32) * grad_scale


def finish(*refs):
    half = len(refs) // 2
    for source, target in zip(refs[:half], refs[half:]):
        target[...] = source[...]


def place_tables(levels, lat_rows, lon_cols, columns):
    grid = np.indices((2, 2, lat_rows // 2, lon_cols // 2, levels)).reshape(5, -1)
    rows = grid.shape[1]
    each = np.arange(rows)
    turned = (grid[4] - WIN_LEV // 2) % levels
    lat_pos = grid[0] * (lat_rows // 2) + grid[2]
    lon_pos = grid[1] * (lon_cols // 2) + grid[3]
    groups = levels // WIN_LEV * REGIONS
    depth = 3 * PLACES + groups
    base = np.zeros((rows, 2 * depth), np.float32)
    for start in range(0, 3 * PLACES, PLACES):
        for half in (0, depth):
            base[each, half + start + turned % WIN_LEV] = 1
            base[each, half + start + WIN_LEV + lat_pos] = 1
            base[each, half + start + SPOT + lon_pos] = 1
    picker = np.zeros((rows, levels * lat_rows + 8), np.float32)
    picker[each, lat_pos * levels + turned] = 1
    picker[each, levels * lat_rows] = turned // WIN_LEV * REGIONS

    place = np.arange(PLACES)
    axis = np.where(place < WIN_LEV, 0, np.where(place < SPOT, 1, 2))
    pos = place - np.array([0, WIN_LEV, SPOT])[axis]
    zero = np.array(
        [WIN_LEV - 1, 2 * WIN_LEV - 1 + WIN_LAT - 1, 2 * WIN_LEV + 2 * WIN_LAT - 2 + WIN_LON - 1]
    )[axis]
    col = np.where(axis[:, None] == axis[None], zero[:, None] + pos[None] - pos[:, None], -1)
    lane = np.arange(HEADS * depth)
    head = (lane // depth) ^ 1
    kind = lane % depth // PLACES
    inside = kind < 3
    cols = np.full((PLACES + 4, HEADS * depth), -1, np.int32)
    cols[:PLACES, inside] = col[:, lane[inside] % depth % PLACES]
    chosen = np.zeros((3 * HEADS, HEADS * depth), np.float32)
    chosen[kind[inside] * HEADS + head[inside], lane[inside]] = 1
    walls = np.zeros((2 * depth, HEADS * depth), np.float32)
    for group in range(groups):
        other = ~inside & (lane % depth - 3 * PLACES != group)
        walls[3 * PLACES + group, other] = barred
    return (
        jnp.asarray(base, bf16),
        jnp.asarray(picker, bf16),
        jnp.asarray(chosen, bf16),
        jnp.asarray(cols),
        jnp.asarray(walls, bf16),
    )


def on_device(
    n_lat,
    n_lon,
    latent,
    cotangent,
    mask_ids,
    position_bias,
    norm_gain,
    w_qkv,
    qkv_down,
    qkv_up,
    w_proj,
    proj_down,
    proj_up,
):
    levels, lat_rows, lon_cols, width = latent.shape
    assert lat_rows == WIN_LAT and lon_cols == WIN_LON
    rows = levels * lat_rows * lon_cols
    part = rows // 4
    rank = qkv_down.shape[0]
    n = n_lat * n_lon
    tables = place_tables(levels, lat_rows, lon_cols, position_bias.shape[1])
    blocks = rank // 8 * (6 * width // 128)
    reduce_here = blocks % n == 0
    own = blocks // n if reduce_here else 1
    peers = n - 1 if reduce_here else 1
    grad_scale = 1.0 / math.sqrt(rows * n)
    grid_shape = jax.ShapeDtypeStruct((lat_rows, lon_cols, levels, width), bf16)
    slab = (lat_rows // 2, lon_cols // 2, levels, width)
    in_place = pl.BlockSpec(memory_space=pl.ANY)
    shapes = (
        grid_shape,
        grid_shape,
        jax.ShapeDtypeStruct((rank, width), f32),
        jax.ShapeDtypeStruct((rank, 3 * width), f32),
        jax.ShapeDtypeStruct((rank, width), f32),
        jax.ShapeDtypeStruct((rank, width), f32),
    )
    in_vmem = pl.BlockSpec(memory_space=pltpu.VMEM)
    dma = pltpu.SemaphoreType.DMA
    results = pl.pallas_call(
        functools.partial(kernel, n_lat, n_lon, reduce_here, grad_scale),
        out_shape=shapes,
        in_specs=[
            in_place if index in (0, 1, 10, 13) else in_vmem for index in range(16)
        ],
        out_specs=[in_vmem] * 6,
        scratch_shapes=[
            pltpu.VMEM(slab, bf16),
            pltpu.VMEM(slab, bf16),
            pltpu.VMEM((3, *slab), bf16),
            pltpu.VMEM((3, *slab), bf16),
            pltpu.VMEM((rows, width), f32),
            pltpu.VMEM((rows, width), f32),
            pltpu.VMEM((rows, width), bf16),
            pltpu.VMEM((rows, 3 * width), bf16),
            pltpu.VMEM((rows, width), bf16),
            pltpu.VMEM((rows, width), bf16),
            pltpu.VMEM((rows, width), bf16),
            pltpu.VMEM((rows, 3 * width), bf16),
            pltpu.VMEM((HEADS, rows, rows), f32),
            pltpu.VMEM((3, *slab), bf16),
            pltpu.VMEM((3, *slab), bf16),
            pltpu.VMEM((blocks, 8, 128), bf16),
            pltpu.VMEM((peers, own, 8, 128), bf16),
            pltpu.VMEM((blocks, 8, 128), bf16),
            pltpu.VMEM((rows, 128), bf16),
            pltpu.VMEM((128, HEADS * 64), f32),
            pltpu.VMEM((levels * lat_rows + 8, 128), f32),
            pltpu.VMEM((width, 3 * width), bf16),
            pltpu.VMEM((width, width), bf16),
            dma((2, 3)),
            dma((2, 3)),
            dma((2, 3)),
            dma((2, 3)),
            dma((peers,)),
            dma((peers,)),
            dma((peers,)),
            dma((peers,)),
            dma((4,)),
        ],
        compiler_params=pltpu.CompilerParams(
            collective_id=0, has_side_effects=True, vmem_limit_bytes=60 * 2**20
        ),
        name="sublayer",
    )(
        latent.transpose(1, 2, 0, 3),
        cotangent.transpose(1, 2, 0, 3),
        mask_ids.transpose(1, 0, 2),
        position_bias,
        *tables,
        norm_gain.reshape(1, width),
        w_qkv,
        qkv_down,
        qkv_up,
        w_proj,
        proj_down,
        proj_up,
    )
    if not reduce_here:
        grads = lax.psum(tuple(results[2:]), ("lon", "lat"))
        results = (*results[:2], *grads)
    output, latent_grad, *grads = pl.pallas_call(
        finish,
        out_shape=shapes,
        in_specs=[in_vmem] * 6,
        out_specs=[in_vmem] * 6,
        name="finish",
    )(*results)
    return (output.transpose(2, 0, 1, 3), latent_grad.transpose(2, 0, 1, 3), *grads)


def solution(mesh):
    return jax.shard_map(
        functools.partial(on_device, mesh.shape["lat"], mesh.shape["lon"]),
        mesh=mesh,
        in_specs=(
            P("runs", "lat", "lon", None),
            P("runs", "lat", "lon", None),
            P("runs", "lat", "lon"),
            P(),
            P(),
            P(),
            P(),
            P(),
            P(),
            P(),
            P(),
        ),
        out_specs=(
            P("runs", "lat", "lon", None),
            P("runs", "lat", "lon", None),
            P("runs", None),
            P("runs", None),
            P("runs", None),
            P("runs", None),
        ),
        check_vma=False,
    )
```

```python
import functools
import math

import jax
import jax.numpy as jnp
import numpy as np
from jax import lax
from jax.experimental import pallas as pl
from jax.experimental.pallas import tpu as pltpu
from jax.sharding import PartitionSpec as P

HEADS = 8
WIN_LEV = 2
WIN_LAT = 6
WIN_LON = 12
REGIONS = 2
PLACES = WIN_LEV + WIN_LAT + WIN_LON
SPOT = WIN_LEV + WIN_LAT

epsilon = 1e-05
barred = -1e30
MESH = pl.DeviceIdType.MESH
f32 = jnp.float32
bf16 = jnp.bfloat16


def mm(a, b):
    return jnp.dot(a, b, preferred_element_type=f32)


def mm_rows(a, b):
    return lax.dot_general(a, b, (((1,), (1,)), ((), ())), preferred_element_type=f32)


def mm_cols(a, b):
    return lax.dot_general(a, b, (((0,), (0,)), ((), ())), preferred_element_type=f32)


def kernel(n_lat, n_lon, reduce_here, grad_scale, *refs):
    (latent, cotangent, mask_ids, position_bias) = refs[:4]
    (base, picker, chosen, columns, walls) = refs[4:9]
    (gain, w_qkv_far, qkv_down, qkv_up, w_proj_far, proj_down, proj_up) = refs[9:16]
    (out_o, grad_o, qd_o, qu_o, pd_o, pu_o) = refs[16:22]
    (x_own, g_own, x_in, g_in, xf, gf, normed_s, qkv_s, kf_s, attn_s, da_s, dqkv_s, probs_s) = refs[22:35]
    (o_send, b_send, terms, slots, total) = refs[35:40]
    (feat, table, ids_s, w_qkv, w_proj) = refs[40:45]
    (in_send, in_recv, out_send, out_recv, rs_send, rs_recv, ag_send, ag_recv, near_sem) = refs[45:]

    lat, lon = lax.axis_index("lat"), lax.axis_index("lon")
    n = n_lat * n_lon
    me = lat * n_lon + lon

    def near(dlat, dlon):
        return {
            "lat": lax.rem(lat + dlat + n_lat, n_lat),
            "lon": lax.rem(lon + dlon + n_lon, n_lon),
        }

    def far(step):
        other = lax.rem(me + step, n)
        return other, {"lat": other // n_lon, "lon": lax.rem(other, n_lon)}

    lat_rows, lon_cols, levels, width = latent.shape
    half_rows, half_cols = lat_rows // 2, lon_cols // 2
    part = levels * half_rows * half_cols
    rows = 4 * part
    pairs = HEADS // 2
    score_scale = 1.0 / math.sqrt(width // HEADS)

    barrier = pltpu.get_barrier_semaphore()
    if reduce_here:
        for step in range(1, n):
            pl.semaphore_signal(barrier, inc=1, device_id=far(step)[1], device_id_type=MESH)
    else:
        for dlat, dlon in ((0, 1), (1, 0), (1, 1)):
            for sign in (1, -1):
                pl.semaphore_signal(
                    barrier, inc=1, device_id=near(sign * dlat, sign * dlon), device_id_type=MESH
                )

    def corner(grid, quarter):
        return grid.at[
            pl.ds(quarter // 2 * half_rows, half_rows), pl.ds(quarter % 2 * half_cols, half_cols)
        ]

    locals_ = []
    for index, (src, dst) in enumerate(
        (
            (corner(latent, 3), x_own),
            (w_qkv_far, w_qkv),
            (corner(cotangent, 3), g_own),
            (w_proj_far, w_proj),
        )
    ):
        copy = pltpu.make_async_copy(src, dst, near_sem.at[index])
        copy.start()
        locals_.append(copy)

    def unpack(slab, flat, region):
        for row in range(half_rows):
            for col in range(half_cols):
                start = region * part + (row * half_cols + col) * levels
                flat[start : start + levels, :] = slab[row, col].astype(f32)

    pl.semaphore_wait(barrier, n - 1 if reduce_here else 6)

    moves = []
    for kind, (src, dst) in enumerate(((latent, x_in), (cotangent, g_in))):
        row = []
        for quarter in (0, 1, 2):
            copy = pltpu.make_async_remote_copy(
                src_ref=corner(src, quarter),
                dst_ref=dst.at[quarter],
                send_sem=in_send.at[kind, quarter],
                recv_sem=in_recv.at[kind, quarter],
                device_id=near(-1 if quarter // 2 == 0 else 0, -1 if quarter % 2 == 0 else 0),
                device_id_type=MESH,
            )
            copy.start()
            row.append(copy)
        moves.append(row)

    ids_s[...] = jnp.zeros_like(ids_s)
    for row in range(lat_rows):
        start = row * levels
        ids_s[start : start + levels, SPOT : SPOT + lon_cols] = mask_ids[row].astype(f32)
    start = levels * lat_rows
    ids_s[start : start + 1, SPOT : SPOT + lon_cols] = jnp.ones((1, lon_cols), f32)
    spots_f = base[...].astype(f32)
    group = jnp.sum(mm(picker[...], ids_s[...].astype(bf16)) * spots_f, axis=-1, keepdims=True)
    lane = lax.broadcasted_iota(jnp.int32, (rows, 128), 1)
    lane = jnp.where(lane >= 64, lane - 64, lane) - 3 * PLACES
    feat[...] = jnp.where(lane.astype(f32) == group, 1.0, spots_f).astype(bf16)

    bias = position_bias[...]
    high = bias.astype(bf16).astype(f32)
    middle = (bias - high).astype(bf16).astype(f32)
    low = bias - high - middle
    parts = jnp.concatenate((high, middle, low), 0).astype(bf16)
    spread = mm_cols(parts, chosen[...])
    column = lax.broadcasted_iota(jnp.int32, spread.shape, 0)
    table[...] = walls[...].astype(f32)
    for place in range(PLACES):
        hit = column == columns[place : place + 1, :]
        table[place : place + 1, :] = jnp.sum(jnp.where(hit, spread, 0.0), axis=0, keepdims=True)
    kf_s[...] = mm(feat[...], table[...].astype(bf16)).astype(bf16)

    locals_[0].wait()
    unpack(x_own, xf, 0)
    for quarter in (0, 1, 2):
        moves[0][quarter].wait()
        unpack(x_in.at[quarter], xf, 3 - quarter)

    def norm():
        x = xf[...]
        centered = x - jnp.mean(x, axis=-1, keepdims=True)
        variance = jnp.mean(centered * centered, axis=-1, keepdims=True)
        inv_std = lax.rsqrt(variance + epsilon)
        return centered * inv_std, inv_std

    normed = (norm()[0] * gain[...]).astype(bf16)
    normed_s[...] = normed
    low_qkv = mm_rows(normed, qkv_down[...]).astype(bf16)
    locals_[1].wait()
    qkv_s[...] = (mm(normed, w_qkv[...]) + mm(low_qkv, qkv_up[...])).astype(bf16)

    left = lax.broadcasted_iota(jnp.int32, (rows, 128), 1) < 64

    def pick(a, b):
        return jnp.where(left, a, b)

    def lanes(first, pair):
        return pl.ds(first + pair * 128, 128)

    def forward_pair(pair):
        query = (qkv_s[:, lanes(0, pair)].astype(f32) * score_scale)
        keys = qkv_s[:, lanes(width, pair)].astype(f32)
        values = qkv_s[:, lanes(2 * width, pair)]
        spots = feat[...].astype(f32)
        offsets = kf_s[:, lanes(0, pair)].astype(f32)
        results = []
        for half in range(2):
            if half == 0:
                q_aug, k_aug = pick(query, spots), pick(keys, offsets)
            else:
                q_aug, k_aug = pick(spots, query), pick(offsets, keys)
            scores = mm_rows(q_aug.astype(bf16), k_aug.astype(bf16))
            terms_e = jnp.exp(scores - jnp.max(scores, axis=-1, keepdims=True))
            probs = terms_e / jnp.sum(terms_e, axis=-1, keepdims=True)
            probs_s[2 * pair + half] = probs
            results.append(mm(probs.astype(bf16), values))
        attn_s[:, lanes(0, pair)] = pick(results[0], results[1]).astype(bf16)

    for pair in range(pairs):
        forward_pair(pair)

    attn = attn_s[...]
    low_proj = mm_rows(attn, proj_down[...]).astype(bf16)
    locals_[3].wait()
    out_rows = xf[...] + mm(attn, w_proj[...]) + mm(low_proj, proj_up[...])
    def pack(value, region, slab):
        for row in range(half_rows):
            for col in range(half_cols):
                start = region * part + (row * half_cols + col) * levels
                slab[row, col] = value[start : start + levels].astype(bf16)

    for region in (3, 2, 1):
        pack(out_rows, region, o_send.at[3 - region])

    def send_out(kind, src, dst):
        row = []
        for quarter in (0, 1, 2):
            copy = pltpu.make_async_remote_copy(
                src_ref=src.at[quarter],
                dst_ref=corner(dst, quarter),
                send_sem=out_send.at[kind, quarter],
                recv_sem=out_recv.at[kind, quarter],
                device_id=near(1 if quarter // 2 == 0 else 0, 1 if quarter % 2 == 0 else 0),
                device_id_type=MESH,
            )
            copy.start()
            row.append(copy)
        return row

    out_moves = send_out(0, o_send, out_o)
    pack(out_rows, 0, corner(out_o, 3))

    locals_[2].wait()
    unpack(g_own, gf, 0)
    for quarter in (0, 1, 2):
        moves[1][quarter].wait()
        unpack(g_in.at[quarter], gf, 3 - quarter)
    grad_rows = gf[...].astype(bf16)
    proj_up_raw = mm_cols(low_proj, grad_rows)
    d_low_proj = mm_rows(grad_rows, proj_up[...]).astype(bf16)
    proj_down_raw = mm_cols(d_low_proj, attn)
    da_s[...] = (mm_rows(grad_rows, w_proj[...]) + mm(d_low_proj, proj_down[...])).astype(bf16)

    own = terms.shape[1]
    places = []
    scatter = []

    def place_terms(raws, first, count):
        index = 0
        for raw, out in raws:
            for top in range(0, raw.shape[0], 8):
                for start in range(0, raw.shape[1], 128):
                    owner, slot = index // count, first + index % count
                    terms[owner, slot] = raw[top : top + 8, start : start + 128].astype(bf16)
                    places.append((owner, slot, out, top, start))
                    index += 1
        batch = 0 if first == 0 else 1
        for step in range(1, n):
            other, where = far(step)
            copy = pltpu.make_async_remote_copy(
                src_ref=terms.at[other, pl.ds(first, count)],
                dst_ref=slots.at[step - 1, pl.ds(first, count)],
                send_sem=rs_send.at[batch, step - 1],
                recv_sem=rs_recv.at[batch, step - 1],
                device_id=where,
                device_id_type=MESH,
            )
            copy.start()
            scatter.append(copy)

    if reduce_here:
        place_terms(((proj_down_raw, pd_o), (proj_up_raw, pu_o)), 0, own // 3)

    def backward_pair(pair):
        query = qkv_s[:, lanes(0, pair)]
        keys = qkv_s[:, lanes(width, pair)]
        values = qkv_s[:, lanes(2 * width, pair)]
        d_attn = da_s[:, lanes(0, pair)]
        d_attn32 = d_attn.astype(f32)
        d_q, d_k, d_v = [], [], []
        for half in range(2):
            own = pick(d_attn32, 0.0) if half == 0 else pick(0.0, d_attn32)
            probs = probs_s[2 * pair + half]
            d_probs = mm_rows(own.astype(bf16), values)
            inner = jnp.sum(d_probs * probs, axis=-1, keepdims=True)
            d_scores = (probs * (d_probs - inner) * score_scale).astype(bf16)
            d_v.append(mm_cols(probs.astype(bf16), d_attn))
            d_q.append(mm(d_scores, keys))
            d_k.append(mm_cols(d_scores, query))
        dqkv_s[:, lanes(0, pair)] = pick(d_q[0], d_q[1]).astype(bf16)
        dqkv_s[:, lanes(width, pair)] = pick(d_k[0], d_k[1]).astype(bf16)
        dqkv_s[:, lanes(2 * width, pair)] = pick(d_v[0], d_v[1]).astype(bf16)

    for pair in range(pairs):
        backward_pair(pair)

    d_qkv = dqkv_s[...]
    qkv_up_raw = mm_cols(low_qkv, d_qkv)
    d_low_qkv = mm_rows(d_qkv, qkv_up[...]).astype(bf16)
    qkv_down_raw = mm_cols(d_low_qkv, normed_s[...])

    if reduce_here:
        place_terms(((qkv_down_raw, qd_o), (qkv_up_raw, qu_o)), own // 3, own - own // 3)
    else:
        for raw, out in (
            (qkv_down_raw, qd_o),
            (qkv_up_raw, qu_o),
            (proj_down_raw, pd_o),
            (proj_up_raw, pu_o),
        ):
            out[...] = raw * grad_scale

    d_normed = mm_rows(d_qkv, w_qkv[...]) + mm(d_low_qkv, qkv_down[...])
    d_unit = d_normed * gain[...]
    unit_rows, inv_std = norm()
    back = inv_std * (
        d_unit
        - jnp.mean(d_unit, axis=-1, keepdims=True)
        - unit_rows * jnp.mean(d_unit * unit_rows, axis=-1, keepdims=True)
    )
    grad_in = gf[...] + back
    for region in (3, 2, 1):
        pack(grad_in, region, b_send.at[3 - region])
    back_moves = send_out(1, b_send, grad_o)
    pack(grad_in, 0, corner(grad_o, 3))

    if reduce_here:
        for copy in scatter:
            copy.wait()
        acc = terms[me].astype(f32)
        for step in range(1, n):
            acc = acc + slots[step - 1].astype(f32)
        total[me] = acc.astype(bf16)
        gather = []
        for step in range(1, n):
            copy = pltpu.make_async_remote_copy(
                src_ref=total.at[me],
                dst_ref=total.at[me],
                send_sem=ag_send.at[step - 1],
                recv_sem=ag_recv.at[step - 1],
                device_id=far(step)[1],
                device_id_type=MESH,
            )
            copy.start()
            gather.append(copy)

    for quarter in (0, 1, 2):
        out_moves[quarter].wait()
        back_moves[quarter].wait()

    if reduce_here:
        for step, copy in enumerate(gather, 1):
            copy.wait()
        for owner, slot, out, top, start in places:
            out[top : top + 8, start : start + 128] = total[owner, slot].astype(f32) * grad_scale


def finish(*refs):
    half = len(refs) // 2
    for source, target in zip(refs[:half], refs[half:]):
        target[...] = source[...]


def place_tables(levels, lat_rows, lon_cols, columns):
    grid = np.indices((2, 2, lat_rows // 2, lon_cols // 2, levels)).reshape(5, -1)
    rows = grid.shape[1]
    each = np.arange(rows)
    turned = (grid[4] - WIN_LEV // 2) % levels
    lat_pos = grid[0] * (lat_rows // 2) + grid[2]
    lon_pos = grid[1] * (lon_cols // 2) + grid[3]
    groups = levels // WIN_LEV * REGIONS
    depth = 3 * PLACES + groups
    base = np.zeros((rows, 2 * depth), np.float32)
    for start in range(0, 3 * PLACES, PLACES):
        for half in (0, depth):
            base[each, half + start + turned % WIN_LEV] = 1
            base[each, half + start + WIN_LEV + lat_pos] = 1
            base[each, half + start + SPOT + lon_pos] = 1
    picker = np.zeros((rows, levels * lat_rows + 8), np.float32)
    picker[each, lat_pos * levels + turned] = 1
    picker[each, levels * lat_rows] = turned // WIN_LEV * REGIONS

    place = np.arange(PLACES)
    axis = np.where(place < WIN_LEV, 0, np.where(place < SPOT, 1, 2))
    pos = place - np.array([0, WIN_LEV, SPOT])[axis]
    zero = np.array(
        [WIN_LEV - 1, 2 * WIN_LEV - 1 + WIN_LAT - 1, 2 * WIN_LEV + 2 * WIN_LAT - 2 + WIN_LON - 1]
    )[axis]
    col = np.where(axis[:, None] == axis[None], zero[:, None] + pos[None] - pos[:, None], -1)
    lane = np.arange(HEADS * depth)
    head = (lane // depth) ^ 1
    kind = lane % depth // PLACES
    inside = kind < 3
    cols = np.full((PLACES + 4, HEADS * depth), -1, np.int32)
    cols[:PLACES, inside] = col[:, lane[inside] % depth % PLACES]
    chosen = np.zeros((3 * HEADS, HEADS * depth), np.float32)
    chosen[kind[inside] * HEADS + head[inside], lane[inside]] = 1
    walls = np.zeros((2 * depth, HEADS * depth), np.float32)
    for group in range(groups):
        other = ~inside & (lane % depth - 3 * PLACES != group)
        walls[3 * PLACES + group, other] = barred
    return (
        jnp.asarray(base, bf16),
        jnp.asarray(picker, bf16),
        jnp.asarray(chosen, bf16),
        jnp.asarray(cols),
        jnp.asarray(walls, bf16),
    )


def on_device(
    n_lat,
    n_lon,
    latent,
    cotangent,
    mask_ids,
    position_bias,
    norm_gain,
    w_qkv,
    qkv_down,
    qkv_up,
    w_proj,
    proj_down,
    proj_up,
):
    levels, lat_rows, lon_cols, width = latent.shape
    assert lat_rows == WIN_LAT and lon_cols == WIN_LON
    rows = levels * lat_rows * lon_cols
    part = rows // 4
    rank = qkv_down.shape[0]
    n = n_lat * n_lon
    tables = place_tables(levels, lat_rows, lon_cols, position_bias.shape[1])
    blocks = rank // 8 * (6 * width // 128)
    reduce_here = blocks % (3 * n) == 0
    own = blocks // n if reduce_here else 1
    owners = n if reduce_here else 1
    peers = n - 1 if reduce_here else 1
    grad_scale = 1.0 / math.sqrt(rows * n)
    grid_shape = jax.ShapeDtypeStruct((lat_rows, lon_cols, levels, width), bf16)
    slab = (lat_rows // 2, lon_cols // 2, levels, width)
    in_place = pl.BlockSpec(memory_space=pl.ANY)
    shapes = (
        grid_shape,
        grid_shape,
        jax.ShapeDtypeStruct((rank, width), f32),
        jax.ShapeDtypeStruct((rank, 3 * width), f32),
        jax.ShapeDtypeStruct((rank, width), f32),
        jax.ShapeDtypeStruct((rank, width), f32),
    )
    in_vmem = pl.BlockSpec(memory_space=pltpu.VMEM)
    dma = pltpu.SemaphoreType.DMA
    results = pl.pallas_call(
        functools.partial(kernel, n_lat, n_lon, reduce_here, grad_scale),
        out_shape=shapes,
        in_specs=[
            in_place if index in (0, 1, 10, 13) else in_vmem for index in range(16)
        ],
        out_specs=[in_vmem] * 6,
        scratch_shapes=[
            pltpu.VMEM(slab, bf16),
            pltpu.VMEM(slab, bf16),
            pltpu.VMEM((3, *slab), bf16),
            pltpu.VMEM((3, *slab), bf16),
            pltpu.VMEM((rows, width), f32),
            pltpu.VMEM((rows, width), f32),
            pltpu.VMEM((rows, width), bf16),
            pltpu.VMEM((rows, 3 * width), bf16),
            pltpu.VMEM((rows, width), bf16),
            pltpu.VMEM((rows, width), bf16),
            pltpu.VMEM((rows, width), bf16),
            pltpu.VMEM((rows, 3 * width), bf16),
            pltpu.VMEM((HEADS, rows, rows), f32),
            pltpu.VMEM((3, *slab), bf16),
            pltpu.VMEM((3, *slab), bf16),
            pltpu.VMEM((owners, own, 8, 128), bf16),
            pltpu.VMEM((peers, own, 8, 128), bf16),
            pltpu.VMEM((owners, own, 8, 128), bf16),
            pltpu.VMEM((rows, 128), bf16),
            pltpu.VMEM((128, HEADS * 64), f32),
            pltpu.VMEM((levels * lat_rows + 8, 128), f32),
            pltpu.VMEM((width, 3 * width), bf16),
            pltpu.VMEM((width, width), bf16),
            dma((2, 3)),
            dma((2, 3)),
            dma((2, 3)),
            dma((2, 3)),
            dma((2, peers)),
            dma((2, peers)),
            dma((peers,)),
            dma((peers,)),
            dma((4,)),
        ],
        compiler_params=pltpu.CompilerParams(
            collective_id=0, has_side_effects=True, vmem_limit_bytes=60 * 2**20
        ),
        name="sublayer",
    )(
        latent.transpose(1, 2, 0, 3),
        cotangent.transpose(1, 2, 0, 3),
        mask_ids.transpose(1, 0, 2),
        position_bias,
        *tables,
        norm_gain.reshape(1, width),
        w_qkv,
        qkv_down,
        qkv_up,
        w_proj,
        proj_down,
        proj_up,
    )
    if not reduce_here:
        grads = lax.psum(tuple(results[2:]), ("lon", "lat"))
        results = (*results[:2], *grads)
    output, latent_grad, *grads = pl.pallas_call(
        finish,
        out_shape=shapes,
        in_specs=[in_vmem] * 6,
        out_specs=[in_vmem] * 6,
        name="finish",
    )(*results)
    return (output.transpose(2, 0, 1, 3), latent_grad.transpose(2, 0, 1, 3), *grads)


def solution(mesh):
    return jax.shard_map(
        functools.partial(on_device, mesh.shape["lat"], mesh.shape["lon"]),
        mesh=mesh,
        in_specs=(
            P("runs", "lat", "lon", None),
            P("runs", "lat", "lon", None),
            P("runs", "lat", "lon"),
            P(),
            P(),
            P(),
            P(),
            P(),
            P(),
            P(),
            P(),
        ),
        out_specs=(
            P("runs", "lat", "lon", None),
            P("runs", "lat", "lon", None),
            P("runs", None),
            P("runs", None),
            P("runs", None),
            P("runs", None),
        ),
        check_vma=False,
    )
```
